128 devices in a mesh: dp: 16 (over z, x_lo, core), tensor: 8 (over x_hi, y).
Axes of the slice: x: 4 (x_hi: 2, x_lo: 2; x = x_hi * 2 + x_lo), y: 4, z: 4, core: 2. Of those that a mesh axis runs over, the one named last changes fastest.
Arguments:
- tokens: bfloat16 [12288, 3072], P('dp'), may hold values from -6 to 6
- assign: int32 [12288, 2], P('dp'), may hold values from 0 to 7, as said below
- combine: float32 [12288, 2], P('dp'), may hold values from 0.1 to 1
- cotangent: bfloat16 [12288, 3072], P('dp'), may hold values from -6 to 6
- w_gate: bfloat16 [3072, 8192], P('dp', 'tensor'), may hold values from -0.109375 to 0.109375
- w_up: bfloat16 [3072, 8192], P('dp', 'tensor'), may hold values from -0.109375 to 0.109375
- w_down_t: bfloat16 [3072, 8192], P('dp', 'tensor'), may hold values from -0.0625 to 0.0625
Outputs:
- mixed: bfloat16 [12288, 3072], P('dp', 'tensor')
- input_grad: bfloat16 [12288, 3072], P('dp', 'tensor')
- weight_grad: float32 [12288], P('dp')
- gate_weight_grad: bfloat16 [3072, 8192], P('dp', 'tensor')
- up_weight_grad: bfloat16 [3072, 8192], P('dp', 'tensor')
- down_weight_grad: bfloat16 [3072, 8192], P('dp', 'tensor')
The draws below stay inside these ranges and needn't reach their ends.
Inputs may be any that keep to these rules, and one draw needn't show every extreme that they name: `assign`: each token names 2 different experts. Of the 768 tokens of one index of dp at most 384 name expert 0, and in every draw the tokens of some index of dp name it exactly 384 times.
All inputs are finite; a program needn't handle non-finite values.
Results may differ from the reference program's by a relative error of at most 0.028.
Values may be sent and summed in bfloat16 or wider, within the bound.
A program may use at most 128 MiB of HBM per device.

```python
import jax
import jax.numpy as jnp
from jax import lax

D = 3072
HIDDEN_SIZE = 8192
EXPERTS = 8
TOPK = 2
TOK_DEV = 768
ROWS_CAP = 384
TOKENS = 12288
N_DP = 16
N_TENSOR = 8


def draw_assign(key, part):
    device_total = TOKENS // TOK_DEV
    row_limit = TOK_DEV // 2
    keys = jax.random.split(key, 6)
    routed_counts = jax.random.randint(keys[0], (device_total,), TOK_DEV // 16, row_limit + 1)
    busiest = jax.random.randint(keys[1], (), 0, device_total)
    routed_counts = jnp.where(jnp.arange(device_total) == busiest, row_limit, routed_counts)
    scores = jax.random.randint(keys[2], (device_total, TOK_DEV), 0, 1 << 16) * TOK_DEV
    scores = scores + jnp.arange(TOK_DEV, dtype=jnp.int32)[None, :]
    order = jnp.argsort(scores, axis=1, stable=True)
    ranks = jnp.argsort(order, axis=1, stable=True)
    routed = ranks < routed_counts[:, None]
    other = jax.random.randint(keys[3], (device_total, TOK_DEV), 1, EXPERTS)
    offset = jax.random.randint(keys[4], (device_total, TOK_DEV), 1, EXPERTS - 1)
    second = 1 + (other - 1 + offset) % (EXPERTS - 1)
    slot = jax.random.randint(keys[5], (device_total, TOK_DEV), 0, 2)
    first_col = jnp.where(routed, jnp.where(slot == 0, 0, other), other)
    second_col = jnp.where(routed, jnp.where(slot == 0, other, 0), second)
    return jnp.stack([first_col, second_col], axis=-1).reshape(TOKENS, TOPK).astype(jnp.int32)


def with_spikes(result, own_key, source, target, parts, factor):
    def block_of(position):
        return (jnp.arange(result.shape[position]) // (result.shape[position] // parts)).reshape((-1,) + (1,) * (result.ndim - 1 - position))

    near = jax.random.permutation(own_key, parts)[block_of(target)]
    other_side = (block_of(target) + parts // 2) % parts
    return jnp.where((block_of(source) == near) | (block_of(source) == other_side), factor * result, result)


def block_scale(own_key, shape, shards, least, high):
    level, own = 1.0, jax.random.fold_in(own_key, 6)
    for position, blocks in shards:
        steps = jnp.exp(jax.random.uniform(jax.random.fold_in(own, position), (blocks,), jnp.float32, least / len(shards), high / len(shards)))
        level = level * jnp.repeat(steps, shape[position] // blocks).reshape([-1 if axis == position else 1 for axis in range(len(shape))])
    return level


def centred(stream_key, extent, width, most, cuts=(), kind=jnp.bfloat16):
    values = width * jax.random.normal(stream_key, extent, jnp.float32)
    if cuts:
        values = values * block_scale(stream_key, extent, cuts, -0.22, 0.18)
    return jnp.clip(values, -most, most).astype(kind)


def gaussian_with(own_key, dims, scale, bound, cuts, heavy, kind=jnp.bfloat16):
    entries = scale * jax.random.normal(own_key, dims, jnp.float32)
    if cuts:
        entries = entries * block_scale(own_key, dims, cuts, -0.22, 0.18)
    return jnp.clip(with_spikes(entries, jax.random.fold_in(own_key, 3), *heavy), -bound, bound).astype(kind)


def setup_inputs(seed: int = 0) -> dict:
    arg_keys = jax.random.split(jax.random.key(seed), 8)
    return {
        "tokens": gaussian_with(arg_keys[0], (TOKENS, D), 1.0, 6.0, ((0, 16),), (0, 1, 16, 2.0)),
        "assign": draw_assign(jax.random.fold_in(arg_keys[7], 71), 0),
        "combine": jnp.clip(0.1 + 0.9 * jax.random.uniform(arg_keys[2], (TOKENS, TOPK), jnp.float32) ** block_scale(arg_keys[2], (TOKENS, TOPK), ((0, 16),), -0.2, 0.2), 0.1, 1.0),
        "cotangent": gaussian_with(arg_keys[3], (TOKENS, D), 1.0, 6.0, ((0, 16),), (0, 1, 16, 2.0)),
        "w_gate": centred(arg_keys[4], (D, HIDDEN_SIZE), D ** -0.5, 0.109375, ((0, 16), (1, 8))),
        "w_up": centred(arg_keys[5], (D, HIDDEN_SIZE), D ** -0.5, 0.109375, ((0, 16), (1, 8))),
        "w_down_t": centred(arg_keys[6], (D, HIDDEN_SIZE), HIDDEN_SIZE ** -0.5, 0.0625, ((0, 16), (1, 8))),
    }


def select_rows(assign_block, combine_block, row_limit):
    token_total = assign_block.shape[0]
    expert_hit = assign_block == 0
    routed = jnp.any(expert_hit, axis=1)
    weight = jnp.sum(jnp.where(expert_hit, combine_block, jnp.zeros((), combine_block.dtype)), axis=1)
    place = jnp.cumsum(routed.astype(jnp.int32)) - 1
    match = routed[None, :] & (place[None, :] == jnp.arange(row_limit, dtype=jnp.int32)[:, None])
    positions = jnp.arange(token_total, dtype=jnp.int32)
    row_index = jnp.sum(jnp.where(match, positions[None, :], 0), axis=1).astype(jnp.int32)
    valid = jnp.any(match, axis=1)
    row_weight = jnp.where(valid, weight[row_index], jnp.zeros((), weight.dtype))
    return row_index, valid, row_weight


def grouped_sum(pairs, groups):
    total = None
    for left, right in pairs:
        left_groups = left.astype(jnp.float32).reshape(left.shape[0], groups, -1)
        right_groups = right.astype(jnp.float32).reshape(right.shape[0], groups, -1)
        term = jnp.einsum("rgf,dgf->grd", left_groups, right_groups)
        total = term if total is None else total + term
    rounded = lax.optimization_barrier(total.astype(jnp.bfloat16))
    return jnp.sum(rounded.astype(jnp.float32), axis=0)


def place_rows(rows, valid, row_index, token_total):
    shape = (token_total,) + rows.shape[1:]
    mask = valid.reshape(valid.shape + (1,) * (rows.ndim - 1))
    values = jnp.where(mask, rows.astype(jnp.float32), jnp.zeros((), jnp.float32))
    return jnp.zeros(shape, jnp.float32).at[row_index].add(values)


def reference(tokens, assign, combine, cotangent, w_gate, w_up, w_down_t):
    def device_step(carry, block):
        tok_block, assign_block, combine_block, grad_block = block
        row_index, valid, row_weight = select_rows(assign_block, combine_block, ROWS_CAP)
        keep = valid[:, None]
        rows_in = jnp.where(keep, tok_block[row_index], jnp.zeros((), tok_block.dtype))
        rows_grad = jnp.where(keep, grad_block[row_index], jnp.zeros((), grad_block.dtype))
        gate_pre = jnp.dot(rows_in, w_gate, preferred_element_type=jnp.float32)
        up_pre = jnp.dot(rows_in, w_up, preferred_element_type=jnp.float32)
        sigmoid_gate = jax.nn.sigmoid(gate_pre)
        hidden = (gate_pre * sigmoid_gate * up_pre).astype(jnp.bfloat16)
        expert_sum = grouped_sum(((hidden, w_down_t),), N_TENSOR)
        mixed_rows = (row_weight[:, None] * expert_sum).astype(jnp.bfloat16)
        weight_rows = jnp.sum(rows_grad.astype(jnp.float32) * expert_sum, axis=1)
        out_grad = (row_weight[:, None] * rows_grad.astype(jnp.float32)).astype(jnp.bfloat16)
        hidden_grad = jnp.dot(out_grad, w_down_t, preferred_element_type=jnp.float32)
        gate_grad = (hidden_grad * up_pre * sigmoid_gate * (1.0 + gate_pre * (1.0 - sigmoid_gate))).astype(jnp.bfloat16)
        up_grad = (hidden_grad * gate_pre * sigmoid_gate).astype(jnp.bfloat16)
        input_rows = grouped_sum(((gate_grad, w_gate), (up_grad, w_up)), N_TENSOR).astype(jnp.bfloat16)
        token_total = tok_block.shape[0]
        mixed_block = place_rows(mixed_rows, valid, row_index, token_total).astype(jnp.bfloat16)
        input_block = place_rows(input_rows, valid, row_index, token_total).astype(jnp.bfloat16)
        weight_block = place_rows(weight_rows, valid, row_index, token_total)
        term = jnp.concatenate([
            jnp.dot(rows_in.T, gate_grad, preferred_element_type=jnp.float32),
            jnp.dot(rows_in.T, up_grad, preferred_element_type=jnp.float32),
            jnp.dot(out_grad.T, hidden, preferred_element_type=jnp.float32)], axis=1)
        rounded = lax.optimization_barrier(term.astype(jnp.bfloat16))
        return carry + rounded.astype(jnp.float32), (mixed_block, input_block, weight_block)

    blocks = (tokens.reshape(N_DP, TOK_DEV, D), assign.reshape(N_DP, TOK_DEV, TOPK),
              combine.reshape(N_DP, TOK_DEV, TOPK), cotangent.reshape(N_DP, TOK_DEV, D))
    init = jnp.zeros((D, 3 * HIDDEN_SIZE), jnp.float32)
    grads, outputs = lax.scan(device_step, init, blocks)
    mixed = outputs[0].reshape(TOKENS, D)
    input_grad = outputs[1].reshape(TOKENS, D)
    weight_grad = outputs[2].reshape(TOKENS)
    grads = grads.astype(jnp.bfloat16)
    return (mixed, input_grad, weight_grad, grads[:, :HIDDEN_SIZE], grads[:, HIDDEN_SIZE:2 * HIDDEN_SIZE], grads[:, 2 * HIDDEN_SIZE:])
```

```python
import functools

import jax
import jax.numpy as jnp
from jax import lax
from jax.experimental import pallas as pl
from jax.experimental.pallas import tpu as pltpu
from jax.sharding import PartitionSpec as P

MESH = pl.DeviceIdType.MESH
BF = jnp.bfloat16
F32 = jnp.float32
RING = 4


def nn(a, b):
    return lax.dot_general(a, b, (((1,), (0,)), ((), ())), preferred_element_type=F32)


def nt(a, b):
    return lax.dot_general(a, b, (((1,), (1,)), ((), ())), preferred_element_type=F32)


def kernel(
    asg, cmb, tok, cot, wg, wu, wd,
    mixed, igrad, wgrad, gg, gu, gd,
    sel, selt, rwv, tb, rin, og, pan, gpre, upre, hid, ggr, ugr, tr,
    grd, r1, r2, r3, fin, ub, rx, u1, u2, u3, wx, mst,
    ld_sem, wl_sem, o_sem,
    sa_s, sa_r, pan_s, pan_r, row_s, row_r,
    gs, gr, us, ur, fs, fr, xs, xr, ws, wr,
):
    rows, toks = sel.shape
    width = rin.shape[1]
    half = pan.shape[2]
    blk = r3.shape[2]
    own_rows = wg.shape[0]
    cols = ub.shape[3]
    tile = tb.shape[2]
    panels = (wg, wu, wd)

    i = lax.axis_index("dp")
    t = lax.axis_index("tensor")
    c = i % 2
    x = (i // 2) % 2
    z = i // 4
    y = t % RING
    xh = t // RING
    ox = 1 - x
    oc = 1 - c
    zn, zp = (z + 1) % RING, (z + 3) % RING
    yn, yp = (y + 1) % RING, (y + 3) % RING

    def dp(zz, xx, cc):
        return {"dp": zz * 4 + xx * 2 + cc}

    sib = dp(z, x, oc)
    pair = dp(z, ox, c)
    znext, zprev = dp(zn, x, c), dp(zp, x, c)
    ynext, yprev = {"tensor": xh * RING + yn}, {"tensor": xh * RING + yp}
    far = {"tensor": (1 - xh) * RING + y}
    others = [{"tensor": (t + k) % 8} for k in range(1, 8)]

    def rc(src, dst, s, r, dev):
        return pltpu.make_async_remote_copy(
            src_ref=src, dst_ref=dst, send_sem=s, recv_sem=r, device_id=dev, device_id_type=MESH
        )

    def load(src, k):
        at = pl.multiple_of(k * tile, tile)
        return pltpu.make_async_copy(src.at[:, pl.ds(at, tile)], tb.at[k % 2], ld_sem.at[k % 2])

    load(tok, 0).start()
    load(tok, 1).start()

    own_cols = pl.ds(pl.multiple_of(c * half, half), half)
    sib_cols = pl.ds(pl.multiple_of(oc * half, half), half)
    own_at = pl.ds(pl.multiple_of(i * own_rows, own_rows), own_rows)

    def wlocal(p):
        return pltpu.make_async_copy(panels[p].at[:, own_cols], pan.at[p, own_at, :], wl_sem.at[p])

    for p in range(3):
        wlocal(p).start()

    bar = pltpu.get_barrier_semaphore()
    partners = [sib, pair, znext, zprev] + others
    for dev in partners:
        pl.semaphore_signal(bar, inc=1, device_id=dev, device_id_type=MESH)
    pl.semaphore_wait(bar, len(partners))

    def to_sib(p):
        return rc(panels[p].at[:, sib_cols], pan.at[p, own_at, :], sa_s.at[p], sa_r.at[p], sib)

    for p in range(3):
        to_sib(p).start()

    def region(p, zz, xx):
        return pan.at[p, pl.ds(pl.multiple_of((zz * 2 + xx) * blk, blk), blk), :]

    def psend(p, k, zz, xx, dev):
        ref = region(p, zz, xx)
        return rc(ref, ref, pan_s.at[p, k], pan_r.at[p, zz * 2 + xx], dev)

    def pwait(p, zz, xx):
        psend(p, 0, zz, xx, pair).wait_recv()

    def own_out(p):
        wlocal(p).wait()
        sib_at = pl.ds(pl.multiple_of((i + 1 - 2 * c) * own_rows, own_rows), own_rows)
        rc(panels[p].at[:, sib_cols], pan.at[p, sib_at, :], sa_s.at[p], sa_r.at[p], sib).wait_recv()
        psend(p, 0, z, x, pair).start()
        psend(p, 1, z, x, znext).start()
        psend(p, 2, z, x, zprev).start()

    def pair_on(p):
        pwait(p, z, ox)
        psend(p, 3, z, ox, znext).start()
        psend(p, 4, z, ox, zprev).start()

    def ring_on(p):
        pwait(p, zp, 0)
        psend(p, 5, zp, 0, znext).start()
        pwait(p, zn, 1)
        psend(p, 6, zn, 1, zprev).start()

    def panel_rest(p):
        pwait(p, zp, 1)
        pwait(p, zn, 0)
        pwait(p, (z + 2) % RING, 0)
        pwait(p, (z + 2) % RING, 1)

    own_out(0)
    own_out(1)

    hit = asg[...] == 0
    routed = jnp.max(jnp.where(hit, 1.0, 0.0), axis=0, keepdims=True)
    weight = jnp.sum(jnp.where(hit, cmb[...], 0.0), axis=0, keepdims=True)
    before = lax.broadcasted_iota(jnp.int32, (toks, toks), 0)
    after = lax.broadcasted_iota(jnp.int32, (toks, toks), 1)
    upto = jnp.where(before <= after, 1.0, 0.0).astype(BF)
    place = nn(jnp.broadcast_to(routed, (8, toks)).astype(BF), upto)[0:1, :] - 1.0
    slot = lax.broadcasted_iota(jnp.int32, (rows, toks), 0).astype(F32)
    chosen = jnp.where(slot == place, routed, 0.0)
    rw = jnp.sum(chosen * weight, axis=1, keepdims=True)
    rwv[...] = jnp.broadcast_to(rw, rwv.shape)
    sel[...] = chosen.astype(BF)
    selt[...] = chosen.T.astype(BF)

    mine = pl.ds(pl.multiple_of(c * rows, rows), rows)
    theirs = pl.ds(pl.multiple_of(oc * rows, rows), rows)
    tiles = width // tile

    def rows_send(k, ref, at):
        return rc(ref.at[at, :], ref.at[at, :], row_s.at[k], row_r.at[k], sib)

    @pl.loop(0, tiles)
    def _(k):
        load(tok, k).wait()
        at = pl.ds(pl.multiple_of(k * tile, tile), tile)
        rin[mine, at] = nn(sel[...], tb[k % 2]).astype(BF)

        @pl.when(k + 2 < tiles)
        def _():
            load(tok, k + 2).start()

    rows_send(0, rin, mine).start()
    load(cot, 0).start()
    load(cot, 1).start()
    pair_on(0)
    own_out(2)

    @pl.loop(0, tiles)
    def _(k):
        load(cot, k).wait()
        at = pl.ds(pl.multiple_of(k * tile, tile), tile)
        got = nn(sel[...], tb[k % 2])
        og[mine, at] = (rwv[:, 0:1] * got).astype(BF)

        @pl.when(k + 2 < tiles)
        def _():
            load(cot, k + 2).start()

    rows_send(1, og, mine).start()
    own_t = pl.ds(pl.multiple_of(t * cols, 128), cols)

    def load_cols():
        return pltpu.make_async_copy(cot.at[:, own_t], tb.at[0, :, pl.ds(0, cols)], ld_sem.at[0])

    load_cols().start()
    pair_on(1)
    ring_on(0)
    pair_on(2)
    ring_on(1)

    third = 256
    steps = 2 * rows // third

    def rtile(k):
        return pl.ds(pl.multiple_of(k * third, third), third)

    rows_send(0, rin, theirs).wait_recv()
    panel_rest(0)

    @pl.loop(0, steps)
    def _(k):
        gpre[rtile(k), :] = nn(rin[rtile(k), :], pan[0])

    ring_on(2)
    panel_rest(1)

    @pl.loop(0, steps)
    def _(k):
        u = nn(rin[rtile(k), :], pan[1])
        g = gpre[rtile(k), :]
        upre[rtile(k), :] = u
        hid[rtile(k), :] = (g * jax.nn.sigmoid(g) * u).astype(BF)

    rows_send(1, og, theirs).wait_recv()

    def chunk_at(j):
        return (z + 2 + 3 * j + 3 * (j // 2) + 2 * (j // 3)) % RING

    def terms(p, left, right):
        tr[...] = left[...].T

        @pl.loop(0, RING)
        def _(j):
            q = chunk_at(j)
            at = pl.ds(pl.multiple_of(q * 2 * blk, 2 * blk), 2 * blk)
            got = nn(tr[...], right[:, at])
            grd[p, q * 2] = got[:, :blk].astype(BF)
            grd[p, q * 2 + 1] = got[:, blk:].astype(BF)

    def scatter(src, a1, a2, a3, ssem, rsem, q, pos, side, nxt, prv, mate, at):
        n1, p1, o2 = (pos + 1) % RING, (pos + 3) % RING, (pos + 2) % RING
        other = 1 - side

        def out(k, ref, dst, dev):
            return rc(ref, dst, ssem.at[q, k], rsem.at[q, k], dev)

        lanes = [
            out(0, src.at[q, at(o2, 0)], a1.at[q, 0], nxt),
            out(1, src.at[q, at(o2, 1)], a1.at[q, 1], prv),
            out(2, src.at[q, at(n1, 1)], a2.at[q, 0, 1], nxt),
            out(3, src.at[q, at(p1, 0)], a2.at[q, 1, 0], prv),
            out(4, src.at[q, at(n1, 0)], a2.at[q, 0, 0], nxt),
            out(5, src.at[q, at(p1, 1)], a2.at[q, 1, 1], prv),
            out(6, src.at[q, at(pos, other)], a3.at[q], mate),
        ]

        def got2(d, s):
            ref = a2.at[q, d, s]
            k = 2 + 2 * (1 - s) + d * (4 * s - 1)
            rc(ref, ref, ssem.at[q, 0], rsem.at[q, k], mate).wait_recv()
            return a2[q, d, s].astype(F32)

        def begin():
            for k in range(4):
                lanes[k].start()

        def middle():
            lanes[0].wait_recv()
            src[q, at(n1, 0)] = (src[q, at(n1, 0)].astype(F32) + a1[q, 0].astype(F32)).astype(BF)
            lanes[4].start()
            lanes[1].wait_recv()
            src[q, at(p1, 1)] = (src[q, at(p1, 1)].astype(F32) + a1[q, 1].astype(F32)).astype(BF)
            lanes[5].start()

        def over():
            total = src[q, at(pos, other)].astype(F32) + got2(0, other) + got2(1, other)
            src[q, at(pos, other)] = total.astype(BF)
            lanes[6].start()

        def finish():
            total = src[q, at(pos, side)].astype(F32) + got2(0, side) + got2(1, side)
            lanes[6].wait_recv()
            return total + a3[q].astype(F32)

        def drain():
            for copy in lanes:
                copy.wait_send()

        return begin, middle, over, finish, drain

    grads = [
        scatter(grd, r1, r2, r3, gs, gr, p, z, x, znext, zprev, pair, lambda a, b: a * 2 + b)
        for p in range(3)
    ]
    feats = [
        scatter(ub, u1, u2, u3, us, ur, q, y, xh, ynext, yprev, far, lambda a, b: b * RING + a)
        for q in range(2)
    ]

    terms(2, hid, og)
    grads[2][0]()

    panel_rest(2)

    @pl.loop(0, steps)
    def _(k):
        hg = nn(og[rtile(k), :], pan[2])
        g = gpre[rtile(k), :]
        s = jax.nn.sigmoid(g)
        ggr[rtile(k), :] = (hg * upre[rtile(k), :] * s * (1.0 + g * (1.0 - s))).astype(BF)
        ugr[rtile(k), :] = (hg * g * s).astype(BF)

    grads[2][1]()
    terms(0, ggr, rin)
    grads[0][0]()

    def prow(p, j):
        return pan[p, pl.ds(pl.multiple_of(j * 2 * cols, 2 * cols), 2 * cols), :]

    def share(q, dst):
        return rc(dst, rx.at[q], xs.at[q], xr.at[q], sib)

    @pl.loop(0, 4)
    def _(j):
        got = nt(hid[theirs, :], prow(2, j))
        ub[1, 2 * j] = got[:, :cols].astype(BF)
        ub[1, 2 * j + 1] = got[:, cols:].astype(BF)

    share(0, ub.at[1]).start()
    terms(1, ugr, rin)
    grads[1][0]()
    grads[2][2]()
    grads[0][1]()
    share(0, ub.at[1]).wait_recv()

    @pl.loop(0, 4)
    def _(j):
        got = nt(hid[mine, :], prow(2, j))
        ub[0, 2 * j] = (got[:, :cols] + rx[0, 2 * j].astype(F32)).astype(BF)
        ub[0, 2 * j + 1] = (got[:, cols:] + rx[0, 2 * j + 1].astype(F32)).astype(BF)

    feats[0][0]()

    @pl.loop(0, 4)
    def _(j):
        got = nt(ggr[theirs, :], prow(0, j)) + nt(ugr[theirs, :], prow(1, j))
        rx[0, 2 * j] = got[:, :cols].astype(BF)
        rx[0, 2 * j + 1] = got[:, cols:].astype(BF)

    share(1, rx.at[0]).start()
    grads[1][1]()
    feats[0][1]()
    share(0, ub.at[1]).wait_send()
    share(1, rx.at[0]).wait_recv()

    @pl.loop(0, 4)
    def _(j):
        got = nt(ggr[mine, :], prow(0, j)) + nt(ugr[mine, :], prow(1, j))
        ub[1, 2 * j] = (got[:, :cols] + rx[1, 2 * j].astype(F32)).astype(BF)
        ub[1, 2 * j + 1] = (got[:, cols:] + rx[1, 2 * j + 1].astype(F32)).astype(BF)

    feats[1][0]()
    for p in range(3):
        for k in range(7):
            psend(p, k, z, x, pair).wait_send()

    def stage(p):
        return pan.at[p, 0:blk, :]

    own_part = pl.ds(pl.multiple_of(c * own_rows, own_rows), own_rows)
    sib_part = pl.ds(pl.multiple_of(oc * own_rows, own_rows), own_rows)

    def hand(p, at):
        return rc(pan.at[p, sib_part, :], fin.at[p, :, at], fs.at[p], fr.at[p], sib)

    def give(p):
        pan[p, 0:blk, :] = grads[p][3]().T.astype(BF)
        hand(p, own_cols).start()
        fin[p, :, own_cols] = pan[p, own_part, :]

    outs = (gg, gu, gd)

    def put(k, src, dst):
        return pltpu.make_async_copy(src, dst, o_sem.at[k])

    feats[0][2]()
    feats[1][1]()
    grads[0][2]()
    give(2)

    e = feats[0][3]()
    mrow = (rwv[:, 0:1] * e).astype(BF)
    mst[0] = nn(selt[...], mrow).astype(BF)
    put(3, mst.at[0], mixed).start()
    load_cols().wait()
    g = nn(sel[...], tb[0, :, 0:cols])
    w = jnp.sum(g * e, axis=1, keepdims=True)
    placed = jnp.sum(sel[...].astype(F32) * w, axis=0, keepdims=True)
    wx[t] = jnp.broadcast_to(placed, (8, toks))

    def tell(k, slot):
        return rc(wx.at[slot], wx.at[slot], ws.at[k], wr.at[slot], others[k - 1])

    for k in range(1, 8):
        tell(k, t).start()

    grads[1][2]()
    feats[1][2]()
    give(0)
    irow = feats[1][3]().astype(BF)
    mst[1] = nn(selt[...], irow).astype(BF)
    put(4, mst.at[1], igrad).start()
    for k in range(1, 8):
        tell(k, (t + k) % 8).wait_recv()
    total = wx[0]
    for k in range(1, 8):
        total = total + wx[k]
    wgrad[...] = total
    give(1)
    for n, p in enumerate((2, 0, 1)):
        hand(p, sib_cols).wait_recv()
        put(n, fin.at[p], outs[p]).start()
    for p in range(3):
        to_sib(p).wait_send()
        hand(p, own_cols).wait_send()
        grads[p][4]()
    for q in range(2):
        feats[q][4]()
    share(1, rx.at[0]).wait_send()
    rows_send(0, rin, mine).wait_send()
    rows_send(1, og, mine).wait_send()
    for k in range(1, 8):
        tell(k, t).wait_send()
    put(3, mst.at[0], mixed).wait()
    put(4, mst.at[1], igrad).wait()
    for n, p in enumerate((2, 0, 1)):
        put(n, fin.at[p], outs[p]).wait()


def local(tokens, assign, combine, cotangent, w_gate, w_up, w_down_t):
    toks, width = tokens.shape
    rows = toks // 2
    own_rows, hidden = w_gate.shape
    half = hidden // 2
    blk = width // 8
    cols = width // 8
    dma = pltpu.SemaphoreType.DMA
    vm = pltpu.VMEM
    anyspace = pl.BlockSpec(memory_space=pl.ANY)
    inside = pl.BlockSpec(memory_space=pltpu.VMEM)
    mixed, igrad, wgrad, gg, gu, gd = pl.pallas_call(
        kernel,
        out_shape=(
            jax.ShapeDtypeStruct((toks, cols), BF),
            jax.ShapeDtypeStruct((toks, cols), BF),
            jax.ShapeDtypeStruct((8, toks), F32),
            jax.ShapeDtypeStruct((own_rows, hidden), BF),
            jax.ShapeDtypeStruct((own_rows, hidden), BF),
            jax.ShapeDtypeStruct((own_rows, hidden), BF),
        ),
        in_specs=[inside, inside] + [anyspace] * 5,
        out_specs=(anyspace, anyspace, inside, anyspace, anyspace, anyspace),
        scratch_shapes=[
            vm((rows, toks), BF),
            vm((toks, rows), BF),
            vm((rows, 128), F32),
            vm((2, toks, 512), BF),
            vm((2 * rows, width), BF),
            vm((2 * rows, width), BF),
            vm((3, width, half), BF),
            vm((2 * rows, half), F32),
            vm((2 * rows, half), F32),
            vm((2 * rows, half), BF),
            vm((2 * rows, half), BF),
            vm((2 * rows, half), BF),
            vm((half, 2 * rows), BF),
            vm((3, 8, half, blk), BF),
            vm((3, 2, half, blk), BF),
            vm((3, 2, 2, half, blk), BF),
            vm((3, half, blk), BF),
            vm((3, own_rows, hidden), BF),
            vm((2, 8, rows, cols), BF),
            vm((2, 8, rows, cols), BF),
            vm((2, 2, rows, cols), BF),
            vm((2, 2, 2, rows, cols), BF),
            vm((2, rows, cols), BF),
            vm((8, 8, toks), F32),
            vm((2, toks, cols), BF),
            dma((2,)), dma((3,)), dma((5,)),
            dma((3,)), dma((3,)), dma((3, 7)), dma((3, 8)), dma((2,)), dma((2,)),
            dma((3, 7)), dma((3, 7)), dma((2, 7)), dma((2, 7)),
            dma((3,)), dma((3,)), dma((2,)), dma((2,)), dma((8,)), dma((8,)),
        ],
        compiler_params=pltpu.CompilerParams(
            collective_id=0, has_side_effects=True, vmem_limit_bytes=62 * 1024 * 1024
        ),
    )(assign.T, combine.T, tokens, cotangent, w_gate, w_up, w_down_t)
    return mixed, igrad, wgrad[0], gg, gu, gd


def solution(mesh):
    return jax.shard_map(
        local,
        mesh=mesh,
        in_specs=(
            P("dp", None),
            P("dp", None),
            P("dp", None),
            P("dp", None),
            P("dp", "tensor"),
            P("dp", "tensor"),
            P("dp", "tensor"),
        ),
        out_specs=(
            P("dp", "tensor"),
            P("dp", "tensor"),
            P("dp"),
            P("dp", "tensor"),
            P("dp", "tensor"),
            P("dp", "tensor"),
        ),
        check_vma=False,
    )
```

```python
import functools

import jax
import jax.numpy as jnp
from jax import lax
from jax.experimental import pallas as pl
from jax.experimental.pallas import tpu as pltpu
from jax.sharding import PartitionSpec as P

MESH = pl.DeviceIdType.MESH
BF = jnp.bfloat16
F32 = jnp.float32
RING = 4


def nn(a, b):
    return lax.dot_general(a, b, (((1,), (0,)), ((), ())), preferred_element_type=F32)


def nt(a, b):
    return lax.dot_general(a, b, (((1,), (1,)), ((), ())), preferred_element_type=F32)


def kernel(
    asg, cmb, tok, cot, wg, wu, wd,
    mixed, igrad, wgrad, gg, gu, gd,
    sel, selt, rwv, tb, rin, og, pan, gpre, upre, hid, ggr, ugr, tr,
    grd, r1, r2, r3, b1, b2, b3, fin, ub, rx, u1, u2, u3, wx, mst,
    ld_sem, wl_sem, o_sem,
    sa_s, sa_r, pan_s, pan_r, half_r, row_s, row_r,
    gs, gr, bs, br, us, ur, fs, fr, xs, xr, ws, wr,
):
    rows, toks = sel.shape
    width = rin.shape[1]
    half = pan.shape[2]
    blk = r3.shape[2]
    own_rows = wg.shape[0]
    cols = ub.shape[3]
    tile = tb.shape[2]
    panels = (wg, wu, wd)

    i = lax.axis_index("dp")
    t = lax.axis_index("tensor")
    c = i % 2
    x = (i // 2) % 2
    z = i // 4
    y = t % RING
    xh = t // RING
    ox = 1 - x
    oc = 1 - c
    zn, zp = (z + 1) % RING, (z + 3) % RING
    yn, yp = (y + 1) % RING, (y + 3) % RING

    def dp(zz, xx, cc):
        return {"dp": zz * 4 + xx * 2 + cc}

    sib = dp(z, x, oc)
    pair = dp(z, ox, c)
    znext, zprev = dp(zn, x, c), dp(zp, x, c)
    ynext, yprev = {"tensor": xh * RING + yn}, {"tensor": xh * RING + yp}
    far = {"tensor": (1 - xh) * RING + y}
    others = [{"tensor": (t + k) % 8} for k in range(1, 8)]

    def rc(src, dst, s, r, dev):
        return pltpu.make_async_remote_copy(
            src_ref=src, dst_ref=dst, send_sem=s, recv_sem=r, device_id=dev, device_id_type=MESH
        )

    def load(src, k):
        at = pl.multiple_of(k * tile, tile)
        return pltpu.make_async_copy(src.at[:, pl.ds(at, tile)], tb.at[k % 2], ld_sem.at[k % 2])

    load(tok, 0).start()
    load(tok, 1).start()

    own_cols = pl.ds(pl.multiple_of(c * half, half), half)
    sib_cols = pl.ds(pl.multiple_of(oc * half, half), half)
    own_at = pl.ds(pl.multiple_of(i * own_rows, own_rows), own_rows)

    def wlocal(p):
        return pltpu.make_async_copy(panels[p].at[:, own_cols], pan.at[p, own_at, :], wl_sem.at[p])

    for p in range(3):
        wlocal(p).start()

    bar = pltpu.get_barrier_semaphore()
    partners = [sib, pair, znext, zprev] + others
    for dev in partners:
        pl.semaphore_signal(bar, inc=1, device_id=dev, device_id_type=MESH)
    pl.semaphore_wait(bar, len(partners))

    def to_sib(p):
        return rc(panels[p].at[:, sib_cols], pan.at[p, own_at, :], sa_s.at[p], sa_r.at[p], sib)

    for p in range(3):
        to_sib(p).start()

    def region(p, zz, xx):
        return pan.at[p, pl.ds(pl.multiple_of((zz * 2 + xx) * blk, blk), blk), :]

    def psend(p, k, zz, xx, dev):
        ref = region(p, zz, xx)
        return rc(ref, ref, pan_s.at[p, k], pan_r.at[p, zz * 2 + xx], dev)

    def pwait(p, zz, xx):
        psend(p, 0, zz, xx, pair).wait_recv()

    def own_out(p):
        wlocal(p).wait()
        sib_at = pl.ds(pl.multiple_of((i + 1 - 2 * c) * own_rows, own_rows), own_rows)
        rc(panels[p].at[:, sib_cols], pan.at[p, sib_at, :], sa_s.at[p], sa_r.at[p], sib).wait_recv()
        psend(p, 0, z, x, pair).start()
        psend(p, 1, z, x, znext).start()
        psend(p, 2, z, x, zprev).start()

    def pair_on(p):
        pwait(p, z, ox)
        psend(p, 3, z, ox, znext).start()
        psend(p, 4, z, ox, zprev).start()

    def ring_on(p):
        pwait(p, zp, 0)
        psend(p, 5, zp, 0, znext).start()
        pwait(p, zn, 1)
        psend(p, 6, zn, 1, zprev).start()

    def panel_rest(p):
        pwait(p, zp, 1)
        pwait(p, zn, 0)
        pwait(p, (z + 2) % RING, 0)
        pwait(p, (z + 2) % RING, 1)

    low, high = pl.ds(0, own_rows), pl.ds(own_rows, own_rows)

    def hsend(p, k, zz, n, dev):
        ref = region(p, zz, x).at[low if n == 0 else high, :]
        return rc(ref, ref, pan_s.at[p, k], half_r.at[n], dev)

    def first_ring(p):
        pwait(p, zp, x)
        hsend(p, 5, zp, 0, znext).start()
        psend(p, 3, zp, x, pair).start()
        pwait(p, zn, x)
        hsend(p, 6, zn, 1, zprev).start()
        psend(p, 4, zn, x, pair).start()

    def last_pair(p):
        z2 = (z + 2) % RING
        hsend(p, 5, z2, 0, znext).wait_recv()
        hsend(p, 6, z2, 1, zprev).wait_recv()
        psend(p, 7, z2, x, pair).start()

    def first_rest(p):
        for k in range(4):
            pwait(p, (z + k) % RING, ox)

    own_out(0)
    own_out(1)

    hit = asg[...] == 0
    routed = jnp.max(jnp.where(hit, 1.0, 0.0), axis=0, keepdims=True)
    weight = jnp.sum(jnp.where(hit, cmb[...], 0.0), axis=0, keepdims=True)
    before = lax.broadcasted_iota(jnp.int32, (toks, toks), 0)
    after = lax.broadcasted_iota(jnp.int32, (toks, toks), 1)
    upto = jnp.where(before <= after, 1.0, 0.0).astype(BF)
    place = nn(jnp.broadcast_to(routed, (8, toks)).astype(BF), upto)[0:1, :] - 1.0
    slot = lax.broadcasted_iota(jnp.int32, (rows, toks), 0).astype(F32)
    chosen = jnp.where(slot == place, routed, 0.0)
    rw = jnp.sum(chosen * weight, axis=1, keepdims=True)
    rwv[...] = jnp.broadcast_to(rw, rwv.shape)
    sel[...] = chosen.astype(BF)
    selt[...] = chosen.T.astype(BF)

    mine = pl.ds(pl.multiple_of(c * rows, rows), rows)
    theirs = pl.ds(pl.multiple_of(oc * rows, rows), rows)
    tiles = width // tile

    def rows_send(k, ref, at):
        return rc(ref.at[at, :], ref.at[at, :], row_s.at[k], row_r.at[k], sib)

    @pl.loop(0, tiles)
    def _(k):
        load(tok, k).wait()
        at = pl.ds(pl.multiple_of(k * tile, tile), tile)
        rin[mine, at] = nn(sel[...], tb[k % 2]).astype(BF)

        @pl.when(k + 2 < tiles)
        def _():
            load(tok, k + 2).start()

    rows_send(0, rin, mine).start()
    load(cot, 0).start()
    load(cot, 1).start()
    first_ring(0)
    pair_on(1)
    own_out(2)

    @pl.loop(0, tiles)
    def _(k):
        load(cot, k).wait()
        at = pl.ds(pl.multiple_of(k * tile, tile), tile)
        got = nn(sel[...], tb[k % 2])
        og[mine, at] = (rwv[:, 0:1] * got).astype(BF)

        @pl.when(k + 2 < tiles)
        def _():
            load(cot, k + 2).start()

    rows_send(1, og, mine).start()
    own_t = pl.ds(pl.multiple_of(t * cols, 128), cols)

    def load_cols():
        return pltpu.make_async_copy(cot.at[:, own_t], tb.at[0, :, pl.ds(0, cols)], ld_sem.at[0])

    load_cols().start()
    last_pair(0)
    ring_on(1)
    pair_on(2)

    third = 256
    steps = 2 * rows // third

    def rtile(k):
        return pl.ds(pl.multiple_of(k * third, third), third)

    rows_send(0, rin, theirs).wait_recv()
    first_rest(0)

    @pl.loop(0, steps)
    def _(k):
        gpre[rtile(k), :] = nn(rin[rtile(k), :], pan[0])

    ring_on(2)
    panel_rest(1)

    @pl.loop(0, steps)
    def _(k):
        u = nn(rin[rtile(k), :], pan[1])
        g = gpre[rtile(k), :]
        upre[rtile(k), :] = u
        hid[rtile(k), :] = (g * jax.nn.sigmoid(g) * u).astype(BF)

    rows_send(1, og, theirs).wait_recv()

    def chunk_at(j):
        return (z + 2 + 3 * j + 3 * (j // 2) + 2 * (j // 3)) % RING

    def terms(p, left, right):
        tr[...] = left[...].T

        @pl.loop(0, RING)
        def _(j):
            q = chunk_at(j)
            at = pl.ds(pl.multiple_of(q * 2 * blk, 2 * blk), 2 * blk)
            got = nn(tr[...], right[:, at])
            grd[p, q * 2] = got[:, :blk].astype(BF)
            grd[p, q * 2 + 1] = got[:, blk:].astype(BF)

    def scatter(src, a1, a2, a3, ssem, rsem, q, pos, side, nxt, prv, mate, at):
        n1, p1, o2 = (pos + 1) % RING, (pos + 3) % RING, (pos + 2) % RING
        other = 1 - side

        def out(k, ref, dst, dev):
            return rc(ref, dst, ssem.at[q, k], rsem.at[q, k], dev)

        lanes = [
            out(0, src.at[q, at(o2, 0)], a1.at[q, 0], nxt),
            out(1, src.at[q, at(o2, 1)], a1.at[q, 1], prv),
            out(2, src.at[q, at(n1, 1)], a2.at[q, 0, 1], nxt),
            out(3, src.at[q, at(p1, 0)], a2.at[q, 1, 0], prv),
            out(4, src.at[q, at(n1, 0)], a2.at[q, 0, 0], nxt),
            out(5, src.at[q, at(p1, 1)], a2.at[q, 1, 1], prv),
            out(6, src.at[q, at(pos, other)], a3.at[q], mate),
        ]

        def got2(d, s):
            ref = a2.at[q, d, s]
            k = 2 + 2 * (1 - s) + d * (4 * s - 1)
            rc(ref, ref, ssem.at[q, 0], rsem.at[q, k], mate).wait_recv()
            return a2[q, d, s].astype(F32)

        def begin():
            for k in range(4):
                lanes[k].start()

        def middle():
            lanes[0].wait_recv()
            src[q, at(n1, 0)] = (src[q, at(n1, 0)].astype(F32) + a1[q, 0].astype(F32)).astype(BF)
            lanes[4].start()
            lanes[1].wait_recv()
            src[q, at(p1, 1)] = (src[q, at(p1, 1)].astype(F32) + a1[q, 1].astype(F32)).astype(BF)
            lanes[5].start()

        def over():
            total = src[q, at(pos, other)].astype(F32) + got2(0, other) + got2(1, other)
            src[q, at(pos, other)] = total.astype(BF)
            lanes[6].start()

        def finish():
            total = src[q, at(pos, side)].astype(F32) + got2(0, side) + got2(1, side)
            lanes[6].wait_recv()
            return total + a3[q].astype(F32)

        def drain():
            for copy in lanes:
                copy.wait_send()

        return begin, middle, over, finish, drain

    def scatter_pair(p):
        n1, p1, o2 = (z + 1) % RING, (z + 3) % RING, (z + 2) % RING
        chunks = (o2, n1, p1, z)
        cut = half // 2
        top, bottom = slice(0, cut), slice(cut, 2 * cut)

        def out(k, ref, dst, dev):
            return rc(ref, dst, bs.at[k], br.at[k], dev)

        def own(q):
            return q * 2 + x

        lanes = [out(k, grd.at[p, q * 2 + ox], b1.at[k], pair) for k, q in enumerate(chunks)]
        lanes += [
            out(4, grd.at[p, own(o2), top, :], b2.at[0], znext),
            out(5, grd.at[p, own(o2), bottom, :], b2.at[1], zprev),
            out(6, grd.at[p, own(n1), bottom, :], b3.at[0, bottom, :], znext),
            out(7, grd.at[p, own(p1), top, :], b3.at[1, top, :], zprev),
            out(8, grd.at[p, own(n1), top, :], b3.at[0, top, :], znext),
            out(9, grd.at[p, own(p1), bottom, :], b3.at[1, bottom, :], zprev),
        ]

        def add(k, part, more):
            at = own(chunks[k])
            grd[p, at, part, :] = (grd[p, at, part, :].astype(F32) + more.astype(F32)).astype(BF)

        def begin():
            for k in range(4):
                lanes[k].start()

        def middle():
            lanes[0].wait_recv()
            add(0, slice(None), b1[0])
            lanes[4].start()
            lanes[5].start()
            lanes[1].wait_recv()
            add(1, slice(None), b1[1])
            lanes[6].start()
            lanes[2].wait_recv()
            add(2, slice(None), b1[2])
            lanes[7].start()

        def over():
            lanes[4].wait_recv()
            add(1, top, b2[0])
            lanes[8].start()
            lanes[5].wait_recv()
            add(2, bottom, b2[1])
            lanes[9].start()

        def finish():
            lanes[3].wait_recv()
            total = grd[p, own(z)].astype(F32) + b1[3].astype(F32)
            for k in (6, 8, 7, 9):
                lanes[k].wait_recv()
            return total + b3[0].astype(F32) + b3[1].astype(F32)

        def drain():
            for copy in lanes:
                copy.wait_send()

        return begin, middle, over, finish, drain

    def placed_at(a, b):
        return a * 2 + b

    def ring_grad(p, q):
        src = grd.at[p : p + 1]
        return scatter(
            src, r1.at[q : q + 1], r2.at[q : q + 1], r3.at[q : q + 1], gs.at[q : q + 1],
            gr.at[q : q + 1], 0, z, x, znext, zprev, pair, placed_at,
        )

    grads = [ring_grad(0, 0), scatter_pair(1), ring_grad(2, 1)]
    feats = [
        scatter(ub, u1, u2, u3, us, ur, q, y, xh, ynext, yprev, far, lambda a, b: b * RING + a)
        for q in range(2)
    ]

    terms(2, hid, og)
    grads[2][0]()

    panel_rest(2)

    @pl.loop(0, steps)
    def _(k):
        hg = nn(og[rtile(k), :], pan[2])
        g = gpre[rtile(k), :]
        s = jax.nn.sigmoid(g)
        ggr[rtile(k), :] = (hg * upre[rtile(k), :] * s * (1.0 + g * (1.0 - s))).astype(BF)
        ugr[rtile(k), :] = (hg * g * s).astype(BF)

    terms(1, ugr, rin)
    grads[1][0]()
    grads[2][1]()
    terms(0, ggr, rin)
    grads[0][0]()

    def prow(p, j):
        return pan[p, pl.ds(pl.multiple_of(j * 2 * cols, 2 * cols), 2 * cols), :]

    def share(q, dst):
        return rc(dst, rx.at[q], xs.at[q], xr.at[q], sib)

    @pl.loop(0, 4)
    def _(j):
        got = nt(hid[theirs, :], prow(2, j))
        ub[1, 2 * j] = got[:, :cols].astype(BF)
        ub[1, 2 * j + 1] = got[:, cols:].astype(BF)

    share(0, ub.at[1]).start()
    grads[1][1]()
    share(0, ub.at[1]).wait_recv()

    @pl.loop(0, 4)
    def _(j):
        got = nt(hid[mine, :], prow(2, j))
        ub[0, 2 * j] = (got[:, :cols] + rx[0, 2 * j].astype(F32)).astype(BF)
        ub[0, 2 * j + 1] = (got[:, cols:] + rx[0, 2 * j + 1].astype(F32)).astype(BF)

    feats[0][0]()

    @pl.loop(0, 4)
    def _(j):
        got = nt(ggr[theirs, :], prow(0, j)) + nt(ugr[theirs, :], prow(1, j))
        rx[0, 2 * j] = got[:, :cols].astype(BF)
        rx[0, 2 * j + 1] = got[:, cols:].astype(BF)

    share(1, rx.at[0]).start()
    grads[2][2]()
    grads[0][1]()
    feats[0][1]()
    share(0, ub.at[1]).wait_send()
    share(1, rx.at[0]).wait_recv()

    @pl.loop(0, 4)
    def _(j):
        got = nt(ggr[mine, :], prow(0, j)) + nt(ugr[mine, :], prow(1, j))
        ub[1, 2 * j] = (got[:, :cols] + rx[1, 2 * j].astype(F32)).astype(BF)
        ub[1, 2 * j + 1] = (got[:, cols:] + rx[1, 2 * j + 1].astype(F32)).astype(BF)

    feats[1][0]()
    for p in range(3):
        for k in range(5):
            psend(p, k, z, x, pair).wait_send()
    for k in range(5, 7):
        hsend(0, k, z, 0, znext).wait_send()
        psend(1, k, z, x, pair).wait_send()
        psend(2, k, z, x, pair).wait_send()
    psend(0, 7, z, x, pair).wait_send()

    def stage(p):
        return pan.at[p, 0:blk, :]

    own_part = pl.ds(pl.multiple_of(c * own_rows, own_rows), own_rows)
    sib_part = pl.ds(pl.multiple_of(oc * own_rows, own_rows), own_rows)

    def hand(p, at):
        return rc(pan.at[p, sib_part, :], fin.at[p, :, at], fs.at[p], fr.at[p], sib)

    def give(p):
        pan[p, 0:blk, :] = grads[p][3]().T.astype(BF)
        hand(p, own_cols).start()
        fin[p, :, own_cols] = pan[p, own_part, :]

    outs = (gg, gu, gd)

    def put(k, src, dst):
        return pltpu.make_async_copy(src, dst, o_sem.at[k])

    grads[1][2]()
    feats[0][2]()
    feats[1][1]()
    grads[0][2]()
    give(2)

    e = feats[0][3]()
    mrow = (rwv[:, 0:1] * e).astype(BF)
    mst[0] = nn(selt[...], mrow).astype(BF)
    put(3, mst.at[0], mixed).start()
    load_cols().wait()
    g = nn(sel[...], tb[0, :, 0:cols])
    w = jnp.sum(g * e, axis=1, keepdims=True)
    placed = jnp.sum(sel[...].astype(F32) * w, axis=0, keepdims=True)
    wx[t] = jnp.broadcast_to(placed, (8, toks))

    def tell(k, slot):
        return rc(wx.at[slot], wx.at[slot], ws.at[k], wr.at[slot], others[k - 1])

    for k in range(1, 8):
        tell(k, t).start()

    feats[1][2]()
    give(0)
    irow = feats[1][3]().astype(BF)
    mst[1] = nn(selt[...], irow).astype(BF)
    put(4, mst.at[1], igrad).start()
    for k in range(1, 8):
        tell(k, (t + k) % 8).wait_recv()
    total = wx[0]
    for k in range(1, 8):
        total = total + wx[k]
    wgrad[...] = total
    give(1)
    for n, p in enumerate((2, 0, 1)):
        hand(p, sib_cols).wait_recv()
        put(n, fin.at[p], outs[p]).start()
    for p in range(3):
        to_sib(p).wait_send()
        hand(p, own_cols).wait_send()
        grads[p][4]()
    for q in range(2):
        feats[q][4]()
    share(1, rx.at[0]).wait_send()
    rows_send(0, rin, mine).wait_send()
    rows_send(1, og, mine).wait_send()
    for k in range(1, 8):
        tell(k, t).wait_send()
    put(3, mst.at[0], mixed).wait()
    put(4, mst.at[1], igrad).wait()
    for n, p in enumerate((2, 0, 1)):
        put(n, fin.at[p], outs[p]).wait()


def hand_out(m, a, g, u, d, w, mo, ao, go, uo, do, wo, mb, ab, gb, ub, db, isem, osem):
    srcs, mids, dsts = (m, a, g, u, d), (mb, ab, gb, ub, db), (mo, ao, go, uo, do)
    into = [pltpu.make_async_copy(srcs[k], mids[k], isem.at[k]) for k in range(5)]
    back = [pltpu.make_async_copy(mids[k], dsts[k], osem.at[k]) for k in range(5)]
    for copy in into:
        copy.start()
    wo[...] = w[0, :]
    for k in range(5):
        into[k].wait()
        back[k].start()
    for copy in back:
        copy.wait()


def local(tokens, assign, combine, cotangent, w_gate, w_up, w_down_t):
    toks, width = tokens.shape
    rows = toks // 2
    own_rows, hidden = w_gate.shape
    half = hidden // 2
    blk = width // 8
    cols = width // 8
    dma = pltpu.SemaphoreType.DMA
    vm = pltpu.VMEM
    anyspace = pl.BlockSpec(memory_space=pl.ANY)
    inside = pl.BlockSpec(memory_space=pltpu.VMEM)
    results = pl.pallas_call(
        kernel,
        out_shape=(
            jax.ShapeDtypeStruct((toks, cols), BF),
            jax.ShapeDtypeStruct((toks, cols), BF),
            jax.ShapeDtypeStruct((8, toks), F32),
            jax.ShapeDtypeStruct((own_rows, hidden), BF),
            jax.ShapeDtypeStruct((own_rows, hidden), BF),
            jax.ShapeDtypeStruct((own_rows, hidden), BF),
        ),
        in_specs=[inside, inside] + [anyspace] * 5,
        out_specs=(anyspace, anyspace, inside, anyspace, anyspace, anyspace),
        scratch_shapes=[
            vm((rows, toks), BF),
            vm((toks, rows), BF),
            vm((rows, 128), F32),
            vm((2, toks, 512), BF),
            vm((2 * rows, width), BF),
            vm((2 * rows, width), BF),
            vm((3, width, half), BF),
            vm((2 * rows, half), F32),
            vm((2 * rows, half), F32),
            vm((2 * rows, half), BF),
            vm((2 * rows, half), BF),
            vm((2 * rows, half), BF),
            vm((half, 2 * rows), BF),
            vm((3, 8, half, blk), BF),
            vm((2, 2, half, blk), BF),
            vm((2, 2, 2, half, blk), BF),
            vm((2, half, blk), BF),
            vm((4, half, blk), BF),
            vm((2, half // 2, blk), BF),
            vm((2, half, blk), BF),
            vm((3, own_rows, hidden), BF),
            vm((2, 8, rows, cols), BF),
            vm((2, 8, rows, cols), BF),
            vm((2, 2, rows, cols), BF),
            vm((2, 2, 2, rows, cols), BF),
            vm((2, rows, cols), BF),
            vm((8, 8, toks), F32),
            vm((2, toks, cols), BF),
            dma((2,)), dma((3,)), dma((5,)),
            dma((3,)), dma((3,)), dma((3, 8)), dma((3, 8)), dma((2,)), dma((2,)), dma((2,)),
            dma((2, 7)), dma((2, 7)), dma((10,)), dma((10,)), dma((2, 7)), dma((2, 7)),
            dma((3,)), dma((3,)), dma((2,)), dma((2,)), dma((8,)), dma((8,)),
        ],
        compiler_params=pltpu.CompilerParams(
            collective_id=0, has_side_effects=True, vmem_limit_bytes=62 * 1024 * 1024
        ),
    )(assign.T, combine.T, tokens, cotangent, w_gate, w_up, w_down_t)
    mixed, igrad, wgrad, gg, gu, gd = results
    kept = (mixed, igrad, gg, gu, gd)
    mixed, igrad, gg, gu, gd, wgrad = pl.pallas_call(
        hand_out,
        out_shape=tuple(jax.ShapeDtypeStruct(a.shape, a.dtype) for a in kept)
        + (jax.ShapeDtypeStruct((toks,), F32),),
        in_specs=[anyspace] * 5 + [inside],
        out_specs=(anyspace,) * 5 + (inside,),
        scratch_shapes=[vm(a.shape, a.dtype) for a in kept] + [dma((5,)), dma((5,))],
    )(*kept, wgrad)
    return mixed, igrad, wgrad, gg, gu, gd


def solution(mesh):
    return jax.shard_map(
        local,
        mesh=mesh,
        in_specs=(
            P("dp", None),
            P("dp", None),
            P("dp", None),
            P("dp", None),
            P("dp", "tensor"),
            P("dp", "tensor"),
            P("dp", "tensor"),
        ),
        out_specs=(
            P("dp", "tensor"),
            P("dp", "tensor"),
            P("dp"),
            P("dp", "tensor"),
            P("dp", "tensor"),
            P("dp", "tensor"),
        ),
        check_vma=False,
    )
```

```python
import functools

import jax
import jax.numpy as jnp
from jax import lax
from jax.experimental import pallas as pl
from jax.experimental.pallas import tpu as pltpu
from jax.sharding import PartitionSpec as P

MESH = pl.DeviceIdType.MESH
BF = jnp.bfloat16
F32 = jnp.float32
RING = 4


def nn(a, b):
    return lax.dot_general(a, b, (((1,), (0,)), ((), ())), preferred_element_type=F32)


def nt(a, b):
    return lax.dot_general(a, b, (((1,), (1,)), ((), ())), preferred_element_type=F32)


def kernel(
    asg, cmb, tok, cot, wg, wu, wd,
    mixed, igrad, wgrad, gg, gu, gd,
    sel, selt, rwv, tb, rin, og, pan, gpre, upre, hid, ggr, ugr, tr,
    grd, r1, r2, r3, b1, b2, b3, fin, ub, rx, u1, u2, u3, wx, hgs,
    ld_sem, wl_sem, o_sem,
    sa_s, sa_r, pan_s, pan_r, half_r, row_s, row_r,
    gs, gr, bs, br, us, ur, fs, fr, xs, xr, ws, wr,
):
    rows, toks = sel.shape
    width = rin.shape[1]
    half = pan.shape[2]
    blk = r3.shape[2]
    own_rows = wg.shape[0]
    cols = ub.shape[3]
    tile = tb.shape[2]
    panels = (wg, wu, wd)

    i = lax.axis_index("dp")
    t = lax.axis_index("tensor")
    c = i % 2
    x = (i // 2) % 2
    z = i // 4
    y = t % RING
    xh = t // RING
    ox = 1 - x
    oc = 1 - c
    zn, zp = (z + 1) % RING, (z + 3) % RING
    yn, yp = (y + 1) % RING, (y + 3) % RING

    def dp(zz, xx, cc):
        return {"dp": zz * 4 + xx * 2 + cc}

    sib = dp(z, x, oc)
    pair = dp(z, ox, c)
    znext, zprev = dp(zn, x, c), dp(zp, x, c)
    ynext, yprev = {"tensor": xh * RING + yn}, {"tensor": xh * RING + yp}
    far = {"tensor": (1 - xh) * RING + y}
    others = [{"tensor": (t + k) % 8} for k in range(1, 8)]

    def rc(src, dst, s, r, dev):
        return pltpu.make_async_remote_copy(
            src_ref=src, dst_ref=dst, send_sem=s, recv_sem=r, device_id=dev, device_id_type=MESH
        )

    def load(src, k):
        at = pl.multiple_of(k * tile, tile)
        return pltpu.make_async_copy(src.at[:, pl.ds(at, tile)], tb.at[k % 2], ld_sem.at[k % 2])

    load(tok, 0).start()
    load(tok, 1).start()

    own_cols = pl.ds(pl.multiple_of(c * half, half), half)
    sib_cols = pl.ds(pl.multiple_of(oc * half, half), half)
    own_at = pl.ds(pl.multiple_of(i * own_rows, own_rows), own_rows)

    def wlocal(p):
        return pltpu.make_async_copy(panels[p].at[:, own_cols], pan.at[p, own_at, :], wl_sem.at[p])

    for p in range(3):
        wlocal(p).start()

    bar = pltpu.get_barrier_semaphore()
    partners = [sib, pair, znext, zprev] + others
    for dev in partners:
        pl.semaphore_signal(bar, inc=1, device_id=dev, device_id_type=MESH)
    pl.semaphore_wait(bar, len(partners))

    def to_sib(p):
        return rc(panels[p].at[:, sib_cols], pan.at[p, own_at, :], sa_s.at[p], sa_r.at[p], sib)

    for p in range(3):
        to_sib(p).start()

    def region(p, zz, xx):
        return pan.at[p, pl.ds(pl.multiple_of((zz * 2 + xx) * blk, blk), blk), :]

    def psend(p, k, zz, xx, dev):
        ref = region(p, zz, xx)
        return rc(ref, ref, pan_s.at[p, k], pan_r.at[p, zz * 2 + xx], dev)

    def pwait(p, zz, xx):
        psend(p, 0, zz, xx, pair).wait_recv()

    def own_out(p):
        wlocal(p).wait()
        sib_at = pl.ds(pl.multiple_of((i + 1 - 2 * c) * own_rows, own_rows), own_rows)
        rc(panels[p].at[:, sib_cols], pan.at[p, sib_at, :], sa_s.at[p], sa_r.at[p], sib).wait_recv()
        psend(p, 0, z, x, pair).start()
        psend(p, 1, z, x, znext).start()
        psend(p, 2, z, x, zprev).start()

    def pair_on(p):
        pwait(p, z, ox)
        psend(p, 3, z, ox, znext).start()
        psend(p, 4, z, ox, zprev).start()

    def ring_on(p):
        pwait(p, zp, x)
        psend(p, 5, zp, x, znext).start()
        pwait(p, zn, ox)
        psend(p, 6, zn, ox, zprev).start()

    def panel_rest(p):
        pwait(p, zp, ox)
        pwait(p, zn, x)
        pwait(p, (z + 2) % RING, 0)
        pwait(p, (z + 2) % RING, 1)

    low, high = pl.ds(0, own_rows), pl.ds(own_rows, own_rows)

    def hsend(p, k, zz, n, dev):
        ref = region(p, zz, x).at[low if n == 0 else high, :]
        return rc(ref, ref, pan_s.at[p, k], half_r.at[n], dev)

    def first_ring(p):
        pwait(p, zp, x)
        hsend(p, 5, zp, 0, znext).start()
        psend(p, 3, zp, x, pair).start()
        pwait(p, zn, x)
        hsend(p, 6, zn, 1, zprev).start()
        psend(p, 4, zn, x, pair).start()

    def last_pair(p):
        z2 = (z + 2) % RING
        hsend(p, 5, z2, 0, znext).wait_recv()
        hsend(p, 6, z2, 1, zprev).wait_recv()
        psend(p, 7, z2, x, pair).start()

    def first_rest(p):
        for k in range(4):
            pwait(p, (z + k) % RING, ox)

    own_out(0)
    own_out(1)

    hit = asg[...] == 0
    routed = jnp.max(jnp.where(hit, 1.0, 0.0), axis=0, keepdims=True)
    weight = jnp.sum(jnp.where(hit, cmb[...], 0.0), axis=0, keepdims=True)
    before = lax.broadcasted_iota(jnp.int32, (toks, toks), 0)
    after = lax.broadcasted_iota(jnp.int32, (toks, toks), 1)
    upto = jnp.where(before <= after, 1.0, 0.0).astype(BF)
    place = nn(jnp.broadcast_to(routed, (8, toks)).astype(BF), upto)[0:1, :] - 1.0
    slot = lax.broadcasted_iota(jnp.int32, (rows, toks), 0).astype(F32)
    chosen = jnp.where(slot == place, routed, 0.0)
    rw = jnp.sum(chosen * weight, axis=1, keepdims=True)
    rwv[...] = jnp.broadcast_to(rw, rwv.shape)
    sel[...] = chosen.astype(BF)
    selt[...] = chosen.T.astype(BF)

    mine = pl.ds(pl.multiple_of(c * rows, rows), rows)
    theirs = pl.ds(pl.multiple_of(oc * rows, rows), rows)
    tiles = width // tile

    def rows_send(k, ref, at):
        return rc(ref.at[at, :], ref.at[at, :], row_s.at[k], row_r.at[k], sib)

    @pl.loop(0, tiles)
    def _(k):
        load(tok, k).wait()
        at = pl.ds(pl.multiple_of(k * tile, tile), tile)
        rin[mine, at] = nn(sel[...], tb[k % 2]).astype(BF)

        @pl.when(k + 2 < tiles)
        def _():
            load(tok, k + 2).start()

    rows_send(0, rin, mine).start()
    load(cot, 0).start()
    load(cot, 1).start()
    first_ring(0)
    pair_on(1)
    own_out(2)

    @pl.loop(0, tiles)
    def _(k):
        load(cot, k).wait()
        at = pl.ds(pl.multiple_of(k * tile, tile), tile)
        got = nn(sel[...], tb[k % 2])
        og[mine, at] = (rwv[:, 0:1] * got).astype(BF)

        @pl.when(k + 2 < tiles)
        def _():
            load(cot, k + 2).start()

    rows_send(1, og, mine).start()
    own_t = pl.ds(pl.multiple_of(t * cols, 128), cols)

    def load_cols():
        return pltpu.make_async_copy(cot.at[:, own_t], tb.at[0, :, pl.ds(0, cols)], ld_sem.at[0])

    load_cols().start()
    last_pair(0)
    ring_on(1)
    pair_on(2)

    third = 256
    steps = 2 * rows // third

    def rtile(k):
        return pl.ds(pl.multiple_of(k * third, third), third)

    rows_send(0, rin, theirs).wait_recv()
    first_rest(0)

    @pl.loop(0, steps)
    def _(k):
        gpre[rtile(k), :] = nn(rin[rtile(k), :], pan[0])

    ring_on(2)
    panel_rest(1)

    @pl.loop(0, steps)
    def _(k):
        u = nn(rin[rtile(k), :], pan[1])
        g = gpre[rtile(k), :]
        upre[rtile(k), :] = u
        hid[rtile(k), :] = (g * jax.nn.sigmoid(g) * u).astype(BF)

    rows_send(1, og, theirs).wait_recv()

    def chunk_at(j):
        return (z + 2 + 3 * j + 3 * (j // 2) + 2 * (j // 3)) % RING

    unit = half // 2

    def terms(p, left, right):
        tr[...] = left[...].T

        @pl.loop(0, RING)
        def _(j):
            q = chunk_at(j)
            at = pl.ds(pl.multiple_of(q * 2 * blk, 2 * blk), 2 * blk)
            got = nn(tr[...], right[:, at])
            for h in range(2):
                part = got[h * unit : (h + 1) * unit].astype(BF)
                grd[2 * p + h, q * 2] = part[:, :blk]
                grd[2 * p + h, q * 2 + 1] = part[:, blk:]

    def scatter(src, a1, a2, a3, ssem, rsem, q, pos, side, nxt, prv, mate, at):
        n1, p1, o2 = (pos + 1) % RING, (pos + 3) % RING, (pos + 2) % RING
        other = 1 - side

        def out(k, ref, dst, dev):
            return rc(ref, dst, ssem.at[q, k], rsem.at[q, k], dev)

        lanes = [
            out(0, src.at[q, at(o2, 0)], a1.at[q, 0], nxt),
            out(1, src.at[q, at(o2, 1)], a1.at[q, 1], prv),
            out(2, src.at[q, at(n1, 1)], a2.at[q, 0, 1], nxt),
            out(3, src.at[q, at(p1, 0)], a2.at[q, 1, 0], prv),
            out(4, src.at[q, at(n1, 0)], a2.at[q, 0, 0], nxt),
            out(5, src.at[q, at(p1, 1)], a2.at[q, 1, 1], prv),
            out(6, src.at[q, at(pos, other)], a3.at[q], mate),
        ]

        def got2(d, s):
            ref = a2.at[q, d, s]
            k = 2 + 2 * (1 - s) + d * (4 * s - 1)
            rc(ref, ref, ssem.at[q, 0], rsem.at[q, k], mate).wait_recv()
            return a2[q, d, s].astype(F32)

        def begin():
            for k in range(4):
                lanes[k].start()

        def middle():
            lanes[0].wait_recv()
            src[q, at(n1, 0)] = (src[q, at(n1, 0)].astype(F32) + a1[q, 0].astype(F32)).astype(BF)
            lanes[4].start()
            lanes[1].wait_recv()
            src[q, at(p1, 1)] = (src[q, at(p1, 1)].astype(F32) + a1[q, 1].astype(F32)).astype(BF)
            lanes[5].start()

        def over():
            total = src[q, at(pos, other)].astype(F32) + got2(0, other) + got2(1, other)
            src[q, at(pos, other)] = total.astype(BF)
            lanes[6].start()

        def finish():
            total = src[q, at(pos, side)].astype(F32) + got2(0, side) + got2(1, side)
            lanes[6].wait_recv()
            return total + a3[q].astype(F32)

        def drain():
            for copy in lanes:
                copy.wait_send()

        return begin, middle, over, finish, drain

    def scatter_pair(p, n):
        n1, p1, o2 = (z + 1) % RING, (z + 3) % RING, (z + 2) % RING
        chunks = (o2, n1, p1, z)
        cut = unit // 2
        top, bottom = slice(0, cut), slice(cut, 2 * cut)

        def out(k, ref, dst, dev):
            return rc(ref, dst, bs.at[n, k], br.at[n, k], dev)

        def own(q):
            return q * 2 + x

        lanes = [out(k, grd.at[p, q * 2 + ox], b1.at[n, k], pair) for k, q in enumerate(chunks)]
        lanes += [
            out(4, grd.at[p, own(o2), top, :], b2.at[n, 0], znext),
            out(5, grd.at[p, own(o2), bottom, :], b2.at[n, 1], zprev),
            out(6, grd.at[p, own(n1), bottom, :], b3.at[n, 0, bottom, :], znext),
            out(7, grd.at[p, own(p1), top, :], b3.at[n, 1, top, :], zprev),
            out(8, grd.at[p, own(n1), top, :], b3.at[n, 0, top, :], znext),
            out(9, grd.at[p, own(p1), bottom, :], b3.at[n, 1, bottom, :], zprev),
        ]

        def add(k, part, more):
            at = own(chunks[k])
            grd[p, at, part, :] = (grd[p, at, part, :].astype(F32) + more.astype(F32)).astype(BF)

        def begin():
            for k in range(4):
                lanes[k].start()

        def middle():
            lanes[0].wait_recv()
            add(0, slice(None), b1[n, 0])
            lanes[4].start()
            lanes[5].start()
            lanes[1].wait_recv()
            add(1, slice(None), b1[n, 1])
            lanes[6].start()
            lanes[2].wait_recv()
            add(2, slice(None), b1[n, 2])
            lanes[7].start()

        def over():
            lanes[4].wait_recv()
            add(1, top, b2[n, 0])
            lanes[8].start()
            lanes[5].wait_recv()
            add(2, bottom, b2[n, 1])
            lanes[9].start()

        def finish():
            lanes[3].wait_recv()
            total = grd[p, own(z)].astype(F32) + b1[n, 3].astype(F32)
            for k in (6, 8, 7, 9):
                lanes[k].wait_recv()
            return total + b3[n, 0].astype(F32) + b3[n, 1].astype(F32)

        def drain():
            for copy in lanes:
                copy.wait_send()

        return begin, middle, over, finish, drain

    def placed_at(a, b):
        return a * 2 + b

    def ring_grad(p, q):
        src = grd.at[p : p + 1]
        return scatter(
            src, r1.at[q : q + 1], r2.at[q : q + 1], r3.at[q : q + 1], gs.at[q : q + 1],
            gr.at[q : q + 1], 0, z, x, znext, zprev, pair, placed_at,
        )

    gate_a, gate_b, up_a, up_b, down_a, down_b = (
        ring_grad(0, 0), ring_grad(1, 1), scatter_pair(2, 0),
        ring_grad(3, 2), scatter_pair(4, 1), ring_grad(5, 3),
    )
    feats = [
        scatter(ub, u1, u2, u3, us, ur, q, y, xh, ynext, yprev, far, lambda a, b: b * RING + a)
        for q in range(2)
    ]

    terms(2, hid, og)
    down_a[0]()
    down_b[0]()

    def prow(p, j):
        return pan[p, pl.ds(pl.multiple_of(j * 2 * cols, 2 * cols), 2 * cols), :]

    def share(q, dst):
        return rc(dst, rx.at[q], xs.at[q], xr.at[q], sib)

    def down_chunk(q, first):
        at = pl.ds(pl.multiple_of(q * 2 * blk, 2 * blk), 2 * blk)

        @pl.loop(0, steps)
        def _(k):
            more = nn(og[rtile(k), at], pan[2, at, :])
            hgs[rtile(k), :] = more if first else hgs[rtile(k), :] + more

        got = nt(hid[theirs, :], prow(2, q))
        ub[1, 2 * q] = got[:, :cols].astype(BF)
        ub[1, 2 * q + 1] = got[:, cols:].astype(BF)

    down_chunk(z, True)
    pwait(2, zp, ox)
    down_chunk(zp, False)
    pwait(2, zn, x)
    down_chunk(zn, False)
    down_b[1]()
    pwait(2, (z + 2) % RING, 0)
    pwait(2, (z + 2) % RING, 1)
    down_chunk((z + 2) % RING, False)
    share(0, ub.at[1]).start()

    @pl.loop(0, steps)
    def _(k):
        hg = hgs[rtile(k), :]
        g = gpre[rtile(k), :]
        s = jax.nn.sigmoid(g)
        ggr[rtile(k), :] = (hg * upre[rtile(k), :] * s * (1.0 + g * (1.0 - s))).astype(BF)
        ugr[rtile(k), :] = (hg * g * s).astype(BF)

    terms(0, ggr, rin)
    gate_a[0]()
    share(0, ub.at[1]).wait_recv()

    @pl.loop(0, 4)
    def _(j):
        got = nt(hid[mine, :], prow(2, j))
        ub[0, 2 * j] = (got[:, :cols] + rx[0, 2 * j].astype(F32)).astype(BF)
        ub[0, 2 * j + 1] = (got[:, cols:] + rx[0, 2 * j + 1].astype(F32)).astype(BF)

    feats[0][0]()
    down_b[2]()
    gate_a[1]()
    gate_b[0]()
    down_a[1]()
    terms(1, ugr, rin)
    up_a[0]()
    up_b[0]()

    @pl.loop(0, 4)
    def _(j):
        got = nt(ggr[theirs, :], prow(0, j)) + nt(ugr[theirs, :], prow(1, j))
        rx[0, 2 * j] = got[:, :cols].astype(BF)
        rx[0, 2 * j + 1] = got[:, cols:].astype(BF)

    share(1, rx.at[0]).start()
    gate_a[2]()
    gate_b[1]()
    feats[0][1]()
    share(0, ub.at[1]).wait_send()
    share(1, rx.at[0]).wait_recv()

    @pl.loop(0, 4)
    def _(j):
        got = nt(ggr[mine, :], prow(0, j)) + nt(ugr[mine, :], prow(1, j))
        ub[1, 2 * j] = (got[:, :cols] + rx[1, 2 * j].astype(F32)).astype(BF)
        ub[1, 2 * j + 1] = (got[:, cols:] + rx[1, 2 * j + 1].astype(F32)).astype(BF)

    feats[1][0]()
    down_a[2]()
    gate_b[2]()
    up_b[1]()
    up_a[1]()
    for p in range(3):
        for k in range(5):
            psend(p, k, z, x, pair).wait_send()
    for k in range(5, 7):
        hsend(0, k, z, 0, znext).wait_send()
        psend(1, k, z, x, pair).wait_send()
        psend(2, k, z, x, pair).wait_send()
    psend(0, 7, z, x, pair).wait_send()

    own_part = pl.ds(pl.multiple_of(c * own_rows, own_rows), own_rows)
    sib_part = pl.ds(pl.multiple_of(oc * own_rows, own_rows), own_rows)

    def hand(p, at):
        return rc(pan.at[p, sib_part, :], fin.at[p, :, at], fs.at[p], fr.at[p], sib)

    def give(p, h, piece):
        pan[p, 0:blk, h * unit : (h + 1) * unit] = piece[3]().T.astype(BF)

    def hand_over(p):
        hand(p, own_cols).start()
        fin[p, :, own_cols] = pan[p, own_part, :]

    outs = (gg, gu, gd)

    def put(k, src, dst):
        return pltpu.make_async_copy(src, dst, o_sem.at[k])

    def put_mixed():
        return put(3, tb.at[1, :, pl.ds(0, cols)], mixed)

    def put_igrad():
        return put(4, tb.at[0, :, pl.ds(0, cols)], igrad)

    feats[0][2]()
    up_b[2]()
    up_a[2]()
    feats[1][1]()
    give(2, 0, down_a)
    give(2, 1, down_b)
    hand_over(2)

    e = feats[0][3]()
    mrow = (rwv[:, 0:1] * e).astype(BF)
    tb[1, :, 0:cols] = nn(selt[...], mrow).astype(BF)
    put_mixed().start()
    load_cols().wait()
    g = nn(sel[...], tb[0, :, 0:cols])
    w = jnp.sum(g * e, axis=1, keepdims=True)
    placed = jnp.sum(sel[...].astype(F32) * w, axis=0, keepdims=True)
    wx[t] = jnp.broadcast_to(placed, (8, toks))

    def tell(k, slot):
        return rc(wx.at[slot], wx.at[slot], ws.at[k], wr.at[slot], others[k - 1])

    for k in range(1, 8):
        tell(k, t).start()

    feats[1][2]()
    give(0, 0, gate_a)
    give(0, 1, gate_b)
    hand_over(0)
    give(1, 1, up_b)
    irow = feats[1][3]().astype(BF)
    tb[0, :, 0:cols] = nn(selt[...], irow).astype(BF)
    put_igrad().start()
    for k in range(1, 8):
        tell(k, (t + k) % 8).wait_recv()
    total = wx[0]
    for k in range(1, 8):
        total = total + wx[k]
    wgrad[...] = total
    give(1, 0, up_a)
    hand_over(1)
    for n, p in enumerate((2, 0, 1)):
        hand(p, sib_cols).wait_recv()
        put(n, fin.at[p], outs[p]).start()
    for p in range(3):
        to_sib(p).wait_send()
        hand(p, own_cols).wait_send()
    for piece in (gate_a, gate_b, up_a, up_b, down_a, down_b):
        piece[4]()
    for q in range(2):
        feats[q][4]()
    share(1, rx.at[0]).wait_send()
    rows_send(0, rin, mine).wait_send()
    rows_send(1, og, mine).wait_send()
    for k in range(1, 8):
        tell(k, t).wait_send()
    put_mixed().wait()
    put_igrad().wait()
    for n, p in enumerate((2, 0, 1)):
        put(n, fin.at[p], outs[p]).wait()


def hand_out(m, a, g, u, d, w, mo, ao, go, uo, do, wo, mb, ab, gb, ub, db, isem, osem):
    srcs, mids, dsts = (m, a, g, u, d), (mb, ab, gb, ub, db), (mo, ao, go, uo, do)
    into = [pltpu.make_async_copy(srcs[k], mids[k], isem.at[k]) for k in range(5)]
    back = [pltpu.make_async_copy(mids[k], dsts[k], osem.at[k]) for k in range(5)]
    for copy in into:
        copy.start()
    wo[...] = w[0, :]
    for k in range(5):
        into[k].wait()
        back[k].start()
    for copy in back:
        copy.wait()


def local(tokens, assign, combine, cotangent, w_gate, w_up, w_down_t):
    toks, width = tokens.shape
    rows = toks // 2
    own_rows, hidden = w_gate.shape
    half = hidden // 2
    blk = width // 8
    cols = width // 8
    dma = pltpu.SemaphoreType.DMA
    vm = pltpu.VMEM
    anyspace = pl.BlockSpec(memory_space=pl.ANY)
    inside = pl.BlockSpec(memory_space=pltpu.VMEM)
    results = pl.pallas_call(
        kernel,
        out_shape=(
            jax.ShapeDtypeStruct((toks, cols), BF),
            jax.ShapeDtypeStruct((toks, cols), BF),
            jax.ShapeDtypeStruct((8, toks), F32),
            jax.ShapeDtypeStruct((own_rows, hidden), BF),
            jax.ShapeDtypeStruct((own_rows, hidden), BF),
            jax.ShapeDtypeStruct((own_rows, hidden), BF),
        ),
        in_specs=[inside, inside] + [anyspace] * 5,
        out_specs=(anyspace, anyspace, inside, anyspace, anyspace, anyspace),
        scratch_shapes=[
            vm((rows, toks), BF),
            vm((toks, rows), BF),
            vm((rows, 128), F32),
            vm((2, toks, 512), BF),
            vm((2 * rows, width), BF),
            vm((2 * rows, width), BF),
            vm((3, width, half), BF),
            vm((2 * rows, half), F32),
            vm((2 * rows, half), F32),
            vm((2 * rows, half), BF),
            vm((2 * rows, half), BF),
            vm((2 * rows, half), BF),
            vm((half, 2 * rows), BF),
            vm((6, 8, half // 2, blk), BF),
            vm((4, 2, half // 2, blk), BF),
            vm((4, 2, 2, half // 2, blk), BF),
            vm((4, half // 2, blk), BF),
            vm((2, 4, half // 2, blk), BF),
            vm((2, 2, half // 4, blk), BF),
            vm((2, 2, half // 2, blk), BF),
            vm((3, own_rows, hidden), BF),
            vm((2, 8, rows, cols), BF),
            vm((2, 8, rows, cols), BF),
            vm((2, 2, rows, cols), BF),
            vm((2, 2, 2, rows, cols), BF),
            vm((2, rows, cols), BF),
            vm((8, 8, toks), F32),
            vm((2 * rows, half), F32),
            dma((2,)), dma((3,)), dma((5,)),
            dma((3,)), dma((3,)), dma((3, 8)), dma((3, 8)), dma((2,)), dma((2,)), dma((2,)),
            dma((4, 7)), dma((4, 7)), dma((2, 10)), dma((2, 10)), dma((2, 7)), dma((2, 7)),
            dma((3,)), dma((3,)), dma((2,)), dma((2,)), dma((8,)), dma((8,)),
        ],
        compiler_params=pltpu.CompilerParams(
            collective_id=0, has_side_effects=True, vmem_limit_bytes=62 * 1024 * 1024
        ),
    )(assign.T, combine.T, tokens, cotangent, w_gate, w_up, w_down_t)
    mixed, igrad, wgrad, gg, gu, gd = results
    kept = (mixed, igrad, gg, gu, gd)
    mixed, igrad, gg, gu, gd, wgrad = pl.pallas_call(
        hand_out,
        out_shape=tuple(jax.ShapeDtypeStruct(a.shape, a.dtype) for a in kept)
        + (jax.ShapeDtypeStruct((toks,), F32),),
        in_specs=[anyspace] * 5 + [inside],
        out_specs=(anyspace,) * 5 + (inside,),
        scratch_shapes=[vm(a.shape, a.dtype) for a in kept] + [dma((5,)), dma((5,))],
    )(*kept, wgrad)
    return mixed, igrad, wgrad, gg, gu, gd


def solution(mesh):
    return jax.shard_map(
        local,
        mesh=mesh,
        in_specs=(
            P("dp", None),
            P("dp", None),
            P("dp", None),
            P("dp", None),
            P("dp", "tensor"),
            P("dp", "tensor"),
            P("dp", "tensor"),
        ),
        out_specs=(
            P("dp", "tensor"),
            P("dp", "tensor"),
            P("dp"),
            P("dp", "tensor"),
            P("dp", "tensor"),
            P("dp", "tensor"),
        ),
        check_vma=False,
    )
```

```python
import functools

import jax
import jax.numpy as jnp
from jax import lax
from jax.experimental import pallas as pl
from jax.experimental.pallas import tpu as pltpu
from jax.sharding import PartitionSpec as P

MESH = pl.DeviceIdType.MESH
BF = jnp.bfloat16
F32 = jnp.float32
RING = 4


def nn(a, b):
    return lax.dot_general(a, b, (((1,), (0,)), ((), ())), preferred_element_type=F32)


def nt(a, b):
    return lax.dot_general(a, b, (((1,), (1,)), ((), ())), preferred_element_type=F32)


def kernel(
    asg, cmb, tok, cot, wg, wu, wd,
    mixed, igrad, wgrad, gg, gu, gd,
    sel, selt, rwv, tb, rin, og, pan, gpre, upre, hid, ggr, ugr, tr,
    grd, r1, r2, r3, b1, b2, b3, fin, ub, rx, u1, u2, u3, wx, hgs,
    ld_sem, wl_sem, o_sem,
    sa_s, sa_r, pan_s, pan_r, half_r, row_s, row_r,
    gs, gr, bs, br, us, ur, fs, fr, xs, xr, ws, wr,
):
    rows, toks = sel.shape
    width = rin.shape[1]
    half = pan.shape[2]
    blk = r3.shape[2]
    own_rows = wg.shape[0]
    cols = ub.shape[3]
    tile = tb.shape[2]
    panels = (wg, wu, wd)

    i = lax.axis_index("dp")
    t = lax.axis_index("tensor")
    c = i % 2
    x = (i // 2) % 2
    z = i // 4
    y = t % RING
    xh = t // RING
    ox = 1 - x
    oc = 1 - c
    zn, zp = (z + 1) % RING, (z + 3) % RING
    yn, yp = (y + 1) % RING, (y + 3) % RING

    def dp(zz, xx, cc):
        return {"dp": zz * 4 + xx * 2 + cc}

    sib = dp(z, x, oc)
    pair = dp(z, ox, c)
    znext, zprev = dp(zn, x, c), dp(zp, x, c)
    ynext, yprev = {"tensor": xh * RING + yn}, {"tensor": xh * RING + yp}
    far = {"tensor": (1 - xh) * RING + y}
    others = [{"tensor": (t + k) % 8} for k in range(1, 8)]

    def rc(src, dst, s, r, dev):
        return pltpu.make_async_remote_copy(
            src_ref=src, dst_ref=dst, send_sem=s, recv_sem=r, device_id=dev, device_id_type=MESH
        )

    def load(src, k):
        at = pl.multiple_of(k * tile, tile)
        return pltpu.make_async_copy(src.at[:, pl.ds(at, tile)], tb.at[k % 2], ld_sem.at[k % 2])

    load(tok, 0).start()
    load(tok, 1).start()

    own_cols = pl.ds(pl.multiple_of(c * half, half), half)
    sib_cols = pl.ds(pl.multiple_of(oc * half, half), half)
    own_at = pl.ds(pl.multiple_of(i * own_rows, own_rows), own_rows)

    def wlocal(p):
        return pltpu.make_async_copy(panels[p].at[:, own_cols], pan.at[p, own_at, :], wl_sem.at[p])

    for p in range(3):
        wlocal(p).start()

    bar = pltpu.get_barrier_semaphore()
    partners = [sib, pair, znext, zprev] + others
    for dev in partners:
        pl.semaphore_signal(bar, inc=1, device_id=dev, device_id_type=MESH)
    pl.semaphore_wait(bar, len(partners))

    def to_sib(p):
        return rc(panels[p].at[:, sib_cols], pan.at[p, own_at, :], sa_s.at[p], sa_r.at[p], sib)

    for p in range(3):
        to_sib(p).start()

    def region(p, zz, xx):
        return pan.at[p, pl.ds(pl.multiple_of((zz * 2 + xx) * blk, blk), blk), :]

    def psend(p, k, zz, xx, dev):
        ref = region(p, zz, xx)
        return rc(ref, ref, pan_s.at[p, k], pan_r.at[p, zz * 2 + xx], dev)

    def pwait(p, zz, xx):
        psend(p, 0, zz, xx, pair).wait_recv()

    def own_out(p):
        wlocal(p).wait()
        sib_at = pl.ds(pl.multiple_of((i + 1 - 2 * c) * own_rows, own_rows), own_rows)
        rc(panels[p].at[:, sib_cols], pan.at[p, sib_at, :], sa_s.at[p], sa_r.at[p], sib).wait_recv()
        psend(p, 0, z, x, pair).start()
        psend(p, 1, z, x, znext).start()
        psend(p, 2, z, x, zprev).start()

    def pair_on(p):
        pwait(p, z, ox)
        psend(p, 3, z, ox, znext).start()
        psend(p, 4, z, ox, zprev).start()

    def ring_on(p):
        pwait(p, zp, x)
        psend(p, 5, zp, x, znext).start()
        pwait(p, zn, ox)
        psend(p, 6, zn, ox, zprev).start()

    def panel_rest(p):
        pwait(p, zp, ox)
        pwait(p, zn, x)
        pwait(p, (z + 2) % RING, 0)
        pwait(p, (z + 2) % RING, 1)

    low, high = pl.ds(0, own_rows), pl.ds(own_rows, own_rows)

    def hsend(p, k, zz, n, dev):
        ref = region(p, zz, x).at[low if n == 0 else high, :]
        return rc(ref, ref, pan_s.at[p, k], half_r.at[n], dev)

    def first_ring(p):
        pwait(p, zp, x)
        hsend(p, 5, zp, 0, znext).start()
        psend(p, 3, zp, x, pair).start()
        pwait(p, zn, x)
        hsend(p, 6, zn, 1, zprev).start()
        psend(p, 4, zn, x, pair).start()

    def last_pair(p):
        z2 = (z + 2) % RING
        hsend(p, 5, z2, 0, znext).wait_recv()
        hsend(p, 6, z2, 1, zprev).wait_recv()
        psend(p, 7, z2, x, pair).start()

    def first_rest(p):
        for k in range(4):
            pwait(p, (z + k) % RING, ox)

    own_out(0)
    own_out(1)

    hit = asg[...] == 0
    routed = jnp.max(jnp.where(hit, 1.0, 0.0), axis=0, keepdims=True)
    weight = jnp.sum(jnp.where(hit, cmb[...], 0.0), axis=0, keepdims=True)
    before = lax.broadcasted_iota(jnp.int32, (toks, toks), 0)
    after = lax.broadcasted_iota(jnp.int32, (toks, toks), 1)
    upto = jnp.where(before <= after, 1.0, 0.0).astype(BF)
    place = nn(jnp.broadcast_to(routed, (8, toks)).astype(BF), upto)[0:1, :] - 1.0
    slot = lax.broadcasted_iota(jnp.int32, (rows, toks), 0).astype(F32)
    chosen = jnp.where(slot == place, routed, 0.0)
    rw = jnp.sum(chosen * weight, axis=1, keepdims=True)
    rwv[...] = jnp.broadcast_to(rw, rwv.shape)
    sel[...] = chosen.astype(BF)
    selt[...] = chosen.T.astype(BF)

    mine = pl.ds(pl.multiple_of(c * rows, rows), rows)
    theirs = pl.ds(pl.multiple_of(oc * rows, rows), rows)
    tiles = width // tile

    def rows_send(k, ref, at):
        return rc(ref.at[at, :], ref.at[at, :], row_s.at[k], row_r.at[k], sib)

    @pl.loop(0, tiles)
    def _(k):
        load(tok, k).wait()
        at = pl.ds(pl.multiple_of(k * tile, tile), tile)
        rin[mine, at] = nn(sel[...], tb[k % 2]).astype(BF)

        @pl.when(k + 2 < tiles)
        def _():
            load(tok, k + 2).start()

    rows_send(0, rin, mine).start()
    load(cot, 0).start()
    load(cot, 1).start()
    first_ring(0)
    pair_on(1)
    own_out(2)

    @pl.loop(0, tiles)
    def _(k):
        load(cot, k).wait()
        at = pl.ds(pl.multiple_of(k * tile, tile), tile)
        got = nn(sel[...], tb[k % 2])
        og[mine, at] = (rwv[:, 0:1] * got).astype(BF)

        @pl.when(k + 2 < tiles)
        def _():
            load(cot, k + 2).start()

    rows_send(1, og, mine).start()
    own_t = pl.ds(pl.multiple_of(t * cols, 128), cols)

    def load_cols():
        return pltpu.make_async_copy(cot.at[:, own_t], tb.at[0, :, pl.ds(0, cols)], ld_sem.at[0])

    load_cols().start()
    last_pair(0)
    ring_on(1)
    pair_on(2)

    third = 256
    steps = 2 * rows // third

    def rtile(k):
        return pl.ds(pl.multiple_of(k * third, third), third)

    rows_send(0, rin, theirs).wait_recv()
    first_rest(0)

    @pl.loop(0, steps)
    def _(k):
        gpre[rtile(k), :] = nn(rin[rtile(k), :], pan[0])

    ring_on(2)
    panel_rest(1)

    @pl.loop(0, steps)
    def _(k):
        u = nn(rin[rtile(k), :], pan[1])
        g = gpre[rtile(k), :]
        upre[rtile(k), :] = u
        hid[rtile(k), :] = (g * jax.nn.sigmoid(g) * u).astype(BF)

    rows_send(1, og, theirs).wait_recv()

    def chunk_at(j):
        return (z + 2 + 3 * j + 3 * (j // 2) + 2 * (j // 3)) % RING

    unit = half // 2

    def terms(p, left, right):
        tr[...] = left[...].T

        @pl.loop(0, RING)
        def _(j):
            q = chunk_at(j)
            at = pl.ds(pl.multiple_of(q * 2 * blk, 2 * blk), 2 * blk)
            got = nn(tr[...], right[:, at])
            for h in range(2):
                part = got[h * unit : (h + 1) * unit].astype(BF)
                grd[2 * p + h, q * 2] = part[:, :blk]
                grd[2 * p + h, q * 2 + 1] = part[:, blk:]

    def scatter(src, a1, a2, a3, ssem, rsem, q, pos, side, nxt, prv, mate, at):
        n1, p1, o2 = (pos + 1) % RING, (pos + 3) % RING, (pos + 2) % RING
        other = 1 - side

        def out(k, ref, dst, dev):
            return rc(ref, dst, ssem.at[q, k], rsem.at[q, k], dev)

        lanes = [
            out(0, src.at[q, at(o2, 0)], a1.at[q, 0], nxt),
            out(1, src.at[q, at(o2, 1)], a1.at[q, 1], prv),
            out(2, src.at[q, at(n1, 1)], a2.at[q, 0, 1], nxt),
            out(3, src.at[q, at(p1, 0)], a2.at[q, 1, 0], prv),
            out(4, src.at[q, at(n1, 0)], a2.at[q, 0, 0], nxt),
            out(5, src.at[q, at(p1, 1)], a2.at[q, 1, 1], prv),
            out(6, src.at[q, at(pos, other)], a3.at[q], mate),
        ]

        def got2(d, s):
            ref = a2.at[q, d, s]
            k = 2 + 2 * (1 - s) + d * (4 * s - 1)
            rc(ref, ref, ssem.at[q, 0], rsem.at[q, k], mate).wait_recv()
            return a2[q, d, s].astype(F32)

        def begin():
            for k in range(4):
                lanes[k].start()

        def middle():
            lanes[0].wait_recv()
            src[q, at(n1, 0)] = (src[q, at(n1, 0)].astype(F32) + a1[q, 0].astype(F32)).astype(BF)
            lanes[4].start()
            lanes[1].wait_recv()
            src[q, at(p1, 1)] = (src[q, at(p1, 1)].astype(F32) + a1[q, 1].astype(F32)).astype(BF)
            lanes[5].start()

        def over():
            total = src[q, at(pos, other)].astype(F32) + got2(0, other) + got2(1, other)
            src[q, at(pos, other)] = total.astype(BF)
            lanes[6].start()

        def finish():
            total = src[q, at(pos, side)].astype(F32) + got2(0, side) + got2(1, side)
            lanes[6].wait_recv()
            return total + a3[q].astype(F32)

        def drain():
            for copy in lanes:
                copy.wait_send()

        return begin, middle, over, finish, drain

    def scatter_pair(p, n):
        n1, p1, o2 = (z + 1) % RING, (z + 3) % RING, (z + 2) % RING
        chunks = (o2, n1, p1, z)
        cut = unit // 2
        top, bottom = slice(0, cut), slice(cut, 2 * cut)

        def out(k, ref, dst, dev):
            return rc(ref, dst, bs.at[n, k], br.at[n, k], dev)

        def own(q):
            return q * 2 + x

        lanes = [out(k, grd.at[p, q * 2 + ox], b1.at[n, k], pair) for k, q in enumerate(chunks)]
        lanes += [
            out(4, grd.at[p, own(o2), top, :], b2.at[n, 0], znext),
            out(5, grd.at[p, own(o2), bottom, :], b2.at[n, 1], zprev),
            out(6, grd.at[p, own(n1), bottom, :], b3.at[n, 0, bottom, :], znext),
            out(7, grd.at[p, own(p1), top, :], b3.at[n, 1, top, :], zprev),
            out(8, grd.at[p, own(n1), top, :], b3.at[n, 0, top, :], znext),
            out(9, grd.at[p, own(p1), bottom, :], b3.at[n, 1, bottom, :], zprev),
        ]

        def add(k, part, more):
            at = own(chunks[k])
            grd[p, at, part, :] = (grd[p, at, part, :].astype(F32) + more.astype(F32)).astype(BF)

        def begin():
            for k in range(4):
                lanes[k].start()

        def middle():
            lanes[0].wait_recv()
            add(0, slice(None), b1[n, 0])
            lanes[4].start()
            lanes[5].start()
            lanes[1].wait_recv()
            add(1, slice(None), b1[n, 1])
            lanes[6].start()
            lanes[2].wait_recv()
            add(2, slice(None), b1[n, 2])
            lanes[7].start()

        def over():
            lanes[4].wait_recv()
            add(1, top, b2[n, 0])
            lanes[8].start()
            lanes[5].wait_recv()
            add(2, bottom, b2[n, 1])
            lanes[9].start()

        def finish():
            lanes[3].wait_recv()
            total = grd[p, own(z)].astype(F32) + b1[n, 3].astype(F32)
            for k in (6, 8, 7, 9):
                lanes[k].wait_recv()
            return total + b3[n, 0].astype(F32) + b3[n, 1].astype(F32)

        def drain():
            for copy in lanes:
                copy.wait_send()

        return begin, middle, over, finish, drain

    def placed_at(a, b):
        return a * 2 + b

    def ring_grad(p, q):
        src = grd.at[p : p + 1]
        return scatter(
            src, r1.at[q : q + 1], r2.at[q : q + 1], r3.at[q : q + 1], gs.at[q : q + 1],
            gr.at[q : q + 1], 0, z, x, znext, zprev, pair, placed_at,
        )

    gate_a, gate_b, up_a, up_b, down_a, down_b = (
        ring_grad(0, 0), ring_grad(1, 1), scatter_pair(2, 0),
        ring_grad(3, 2), scatter_pair(4, 1), ring_grad(5, 3),
    )
    feats = [
        scatter(ub, u1, u2, u3, us, ur, q, y, xh, ynext, yprev, far, lambda a, b: b * RING + a)
        for q in range(2)
    ]

    terms(2, hid, og)
    down_a[0]()
    down_b[0]()

    def prow(p, j):
        return pan[p, pl.ds(pl.multiple_of(j * 2 * cols, 2 * cols), 2 * cols), :]

    def share(q, dst):
        return rc(dst, rx.at[q], xs.at[q], xr.at[q], sib)

    def down_chunk(q, first):
        at = pl.ds(pl.multiple_of(q * 2 * blk, 2 * blk), 2 * blk)

        @pl.loop(0, steps)
        def _(k):
            more = nn(og[rtile(k), at], pan[2, at, :])
            hgs[rtile(k), :] = more if first else hgs[rtile(k), :] + more

        got = nt(hid[theirs, :], prow(2, q))
        ub[1, 2 * q] = got[:, :cols].astype(BF)
        ub[1, 2 * q + 1] = got[:, cols:].astype(BF)

    down_chunk(z, True)
    pwait(2, zp, ox)
    down_chunk(zp, False)
    pwait(2, zn, x)
    down_chunk(zn, False)
    down_b[1]()
    pwait(2, (z + 2) % RING, 0)
    pwait(2, (z + 2) % RING, 1)
    down_chunk((z + 2) % RING, False)
    share(0, ub.at[1]).start()

    @pl.loop(0, steps)
    def _(k):
        hg = hgs[rtile(k), :]
        g = gpre[rtile(k), :]
        s = jax.nn.sigmoid(g)
        ggr[rtile(k), :] = (hg * upre[rtile(k), :] * s * (1.0 + g * (1.0 - s))).astype(BF)
        ugr[rtile(k), :] = (hg * g * s).astype(BF)

    terms(0, ggr, rin)
    gate_a[0]()
    share(0, ub.at[1]).wait_recv()

    @pl.loop(0, 4)
    def _(j):
        got = nt(hid[mine, :], prow(2, j))
        ub[0, 2 * j] = (got[:, :cols] + rx[0, 2 * j].astype(F32)).astype(BF)
        ub[0, 2 * j + 1] = (got[:, cols:] + rx[0, 2 * j + 1].astype(F32)).astype(BF)

    feats[0][0]()
    down_b[2]()
    gate_a[1]()
    gate_b[0]()
    down_a[1]()
    terms(1, ugr, rin)
    up_a[0]()
    up_b[0]()

    @pl.loop(0, 4)
    def _(j):
        got = nt(ggr[theirs, :], prow(0, j)) + nt(ugr[theirs, :], prow(1, j))
        rx[0, 2 * j] = got[:, :cols].astype(BF)
        rx[0, 2 * j + 1] = got[:, cols:].astype(BF)

    share(1, rx.at[0]).start()
    gate_a[2]()
    gate_b[1]()
    feats[0][1]()
    share(0, ub.at[1]).wait_send()
    share(1, rx.at[0]).wait_recv()

    @pl.loop(0, 4)
    def _(j):
        got = nt(ggr[mine, :], prow(0, j)) + nt(ugr[mine, :], prow(1, j))
        ub[1, 2 * j] = (got[:, :cols] + rx[1, 2 * j].astype(F32)).astype(BF)
        ub[1, 2 * j + 1] = (got[:, cols:] + rx[1, 2 * j + 1].astype(F32)).astype(BF)

    feats[1][0]()
    down_a[2]()
    gate_b[2]()
    up_b[1]()
    up_a[1]()
    for p in range(3):
        for k in range(5):
            psend(p, k, z, x, pair).wait_send()
    for k in range(5, 7):
        hsend(0, k, z, 0, znext).wait_send()
        psend(1, k, z, x, pair).wait_send()
        psend(2, k, z, x, pair).wait_send()
    psend(0, 7, z, x, pair).wait_send()

    own_part = pl.ds(pl.multiple_of(c * own_rows, own_rows), own_rows)
    sib_part = pl.ds(pl.multiple_of(oc * own_rows, own_rows), own_rows)

    def hand(p, at):
        return rc(pan.at[p, sib_part, :], fin.at[p, :, at], fs.at[p], fr.at[p], sib)

    def give(p, h, piece):
        pan[p, 0:blk, h * unit : (h + 1) * unit] = piece[3]().T.astype(BF)

    def hand_over(p):
        hand(p, own_cols).start()
        fin[p, :, own_cols] = pan[p, own_part, :]

    outs = (gg, gu, gd)

    def put(k, src, dst):
        return pltpu.make_async_copy(src, dst, o_sem.at[k])

    def put_mixed():
        return put(3, tb.at[1, :, pl.ds(0, cols)], mixed)

    def put_igrad():
        return put(4, tb.at[0, :, pl.ds(0, cols)], igrad)

    feats[0][2]()
    up_b[2]()
    up_a[2]()
    feats[1][1]()
    give(2, 0, down_a)
    give(2, 1, down_b)
    hand_over(2)

    e = feats[0][3]()
    mrow = (rwv[:, 0:1] * e).astype(BF)
    tb[1, :, 0:cols] = nn(selt[...], mrow).astype(BF)
    put_mixed().start()
    load_cols().wait()
    g = nn(sel[...], tb[0, :, 0:cols])
    w = jnp.sum(g * e, axis=1, keepdims=True)
    placed = jnp.sum(sel[...].astype(F32) * w, axis=0, keepdims=True)
    wx[t] = jnp.broadcast_to(placed, (8, toks))

    def tell(k, slot):
        return rc(wx.at[slot], wx.at[slot], ws.at[k], wr.at[slot], others[k - 1])

    for k in range(1, 8):
        tell(k, t).start()

    feats[1][2]()
    give(0, 0, gate_a)
    give(0, 1, gate_b)
    hand_over(0)
    give(1, 1, up_b)
    for k in range(1, 8):
        tell(k, (t + k) % 8).wait_recv()
    total = wx[0]
    for k in range(1, 8):
        total = total + wx[k]
    wgrad[...] = total
    give(1, 0, up_a)
    hand_over(1)
    irow = feats[1][3]().astype(BF)
    tb[0, :, 0:cols] = nn(selt[...], irow).astype(BF)
    put_igrad().start()
    for n, p in enumerate((2, 0, 1)):
        hand(p, sib_cols).wait_recv()
        put(n, fin.at[p], outs[p]).start()
    for p in range(3):
        to_sib(p).wait_send()
        hand(p, own_cols).wait_send()
    for piece in (gate_a, gate_b, up_a, up_b, down_a, down_b):
        piece[4]()
    for q in range(2):
        feats[q][4]()
    share(1, rx.at[0]).wait_send()
    rows_send(0, rin, mine).wait_send()
    rows_send(1, og, mine).wait_send()
    for k in range(1, 8):
        tell(k, t).wait_send()
    put_mixed().wait()
    put_igrad().wait()
    for n, p in enumerate((2, 0, 1)):
        put(n, fin.at[p], outs[p]).wait()


def hand_out(m, a, g, u, d, w, mo, ao, go, uo, do, wo, mb, ab, gb, ub, db, isem, osem):
    srcs, mids, dsts = (m, a, g, u, d), (mb, ab, gb, ub, db), (mo, ao, go, uo, do)
    into = [pltpu.make_async_copy(srcs[k], mids[k], isem.at[k]) for k in range(5)]
    back = [pltpu.make_async_copy(mids[k], dsts[k], osem.at[k]) for k in range(5)]
    for copy in into:
        copy.start()
    wo[...] = w[0, :]
    for k in range(5):
        into[k].wait()
        back[k].start()
    for copy in back:
        copy.wait()


def local(tokens, assign, combine, cotangent, w_gate, w_up, w_down_t):
    toks, width = tokens.shape
    rows = toks // 2
    own_rows, hidden = w_gate.shape
    half = hidden // 2
    blk = width // 8
    cols = width // 8
    dma = pltpu.SemaphoreType.DMA
    vm = pltpu.VMEM
    anyspace = pl.BlockSpec(memory_space=pl.ANY)
    inside = pl.BlockSpec(memory_space=pltpu.VMEM)
    results = pl.pallas_call(
        kernel,
        out_shape=(
            jax.ShapeDtypeStruct((toks, cols), BF),
            jax.ShapeDtypeStruct((toks, cols), BF),
            jax.ShapeDtypeStruct((8, toks), F32),
            jax.ShapeDtypeStruct((own_rows, hidden), BF),
            jax.ShapeDtypeStruct((own_rows, hidden), BF),
            jax.ShapeDtypeStruct((own_rows, hidden), BF),
        ),
        in_specs=[inside, inside] + [anyspace] * 5,
        out_specs=(anyspace, anyspace, inside, anyspace, anyspace, anyspace),
        scratch_shapes=[
            vm((rows, toks), BF),
            vm((toks, rows), BF),
            vm((rows, 128), F32),
            vm((2, toks, 512), BF),
            vm((2 * rows, width), BF),
            vm((2 * rows, width), BF),
            vm((3, width, half), BF),
            vm((2 * rows, half), F32),
            vm((2 * rows, half), F32),
            vm((2 * rows, half), BF),
            vm((2 * rows, half), BF),
            vm((2 * rows, half), BF),
            vm((half, 2 * rows), BF),
            vm((6, 8, half // 2, blk), BF),
            vm((4, 2, half // 2, blk), BF),
            vm((4, 2, 2, half // 2, blk), BF),
            vm((4, half // 2, blk), BF),
            vm((2, 4, half // 2, blk), BF),
            vm((2, 2, half // 4, blk), BF),
            vm((2, 2, half // 2, blk), BF),
            vm((3, own_rows, hidden), BF),
            vm((2, 8, rows, cols), BF),
            vm((2, 8, rows, cols), BF),
            vm((2, 2, rows, cols), BF),
            vm((2, 2, 2, rows, cols), BF),
            vm((2, rows, cols), BF),
            vm((8, 8, toks), F32),
            vm((2 * rows, half), F32),
            dma((2,)), dma((3,)), dma((5,)),
            dma((3,)), dma((3,)), dma((3, 8)), dma((3, 8)), dma((2,)), dma((2,)), dma((2,)),
            dma((4, 7)), dma((4, 7)), dma((2, 10)), dma((2, 10)), dma((2, 7)), dma((2, 7)),
            dma((3,)), dma((3,)), dma((2,)), dma((2,)), dma((8,)), dma((8,)),
        ],
        compiler_params=pltpu.CompilerParams(
            collective_id=0, has_side_effects=True, vmem_limit_bytes=62 * 1024 * 1024
        ),
    )(assign.T, combine.T, tokens, cotangent, w_gate, w_up, w_down_t)
    mixed, igrad, wgrad, gg, gu, gd = results
    kept = (mixed, igrad, gg, gu, gd)
    mixed, igrad, gg, gu, gd, wgrad = pl.pallas_call(
        hand_out,
        out_shape=tuple(jax.ShapeDtypeStruct(a.shape, a.dtype) for a in kept)
        + (jax.ShapeDtypeStruct((toks,), F32),),
        in_specs=[anyspace] * 5 + [inside],
        out_specs=(anyspace,) * 5 + (inside,),
        scratch_shapes=[vm(a.shape, a.dtype) for a in kept] + [dma((5,)), dma((5,))],
    )(*kept, wgrad)
    return mixed, igrad, wgrad, gg, gu, gd


def solution(mesh):
    return jax.shard_map(
        local,
        mesh=mesh,
        in_specs=(
            P("dp", None),
            P("dp", None),
            P("dp", None),
            P("dp", None),
            P("dp", "tensor"),
            P("dp", "tensor"),
            P("dp", "tensor"),
        ),
        out_specs=(
            P("dp", "tensor"),
            P("dp", "tensor"),
            P("dp"),
            P("dp", "tensor"),
            P("dp", "tensor"),
            P("dp", "tensor"),
        ),
        check_vma=False,
    )
```

```python
import functools

import jax
import jax.numpy as jnp
from jax import lax
from jax.experimental import pallas as pl
from jax.experimental.pallas import tpu as pltpu
from jax.sharding import PartitionSpec as P

MESH = pl.DeviceIdType.MESH
BF = jnp.bfloat16
F32 = jnp.float32
RING = 4


def nn(a, b):
    return lax.dot_general(a, b, (((1,), (0,)), ((), ())), preferred_element_type=F32)


def nt(a, b):
    return lax.dot_general(a, b, (((1,), (1,)), ((), ())), preferred_element_type=F32)


def kernel(
    asg, cmb, tok, cot, wg, wu, wd,
    mixed, igrad, wgrad, gg, gu, gd,
    sel, selt, rwv, tb, rin, og, pan, gpre, upre, hid, ggr, ugr, tr,
    grd, r1, r2, r3, b1, b2, b3, fin, ub, rx, u1, u2, u3, wx, hgs,
    ld_sem, wl_sem, o_sem,
    sa_s, sa_r, pan_s, pan_r, half_r, row_s, row_r,
    gs, gr, bs, br, us, ur, fs, fr, xs, xr, ws, wr,
):
    rows, toks = sel.shape
    width = rin.shape[1]
    half = pan.shape[2]
    blk = r3.shape[2]
    own_rows = wg.shape[0]
    cols = ub.shape[3]
    tile = tb.shape[2]
    panels = (wg, wu, wd)

    i = lax.axis_index("dp")
    t = lax.axis_index("tensor")
    c = i % 2
    x = (i // 2) % 2
    z = i // 4
    y = t % RING
    xh = t // RING
    ox = 1 - x
    oc = 1 - c
    zn, zp = (z + 1) % RING, (z + 3) % RING
    yn, yp = (y + 1) % RING, (y + 3) % RING

    def dp(zz, xx, cc):
        return {"dp": zz * 4 + xx * 2 + cc}

    sib = dp(z, x, oc)
    pair = dp(z, ox, c)
    znext, zprev = dp(zn, x, c), dp(zp, x, c)
    ynext, yprev = {"tensor": xh * RING + yn}, {"tensor": xh * RING + yp}
    far = {"tensor": (1 - xh) * RING + y}
    others = [{"tensor": (t + k) % 8} for k in range(1, 8)]

    def rc(src, dst, s, r, dev):
        return pltpu.make_async_remote_copy(
            src_ref=src, dst_ref=dst, send_sem=s, recv_sem=r, device_id=dev, device_id_type=MESH
        )

    def load(src, k):
        at = pl.multiple_of(k * tile, tile)
        return pltpu.make_async_copy(src.at[:, pl.ds(at, tile)], tb.at[k % 2], ld_sem.at[k % 2])

    load(tok, 0).start()
    load(tok, 1).start()

    own_cols = pl.ds(pl.multiple_of(c * half, half), half)
    sib_cols = pl.ds(pl.multiple_of(oc * half, half), half)
    own_at = pl.ds(pl.multiple_of(i * own_rows, own_rows), own_rows)

    def wlocal(p):
        return pltpu.make_async_copy(panels[p].at[:, own_cols], pan.at[p, own_at, :], wl_sem.at[p])

    for p in range(3):
        wlocal(p).start()

    bar = pltpu.get_barrier_semaphore()
    partners = [sib, pair, znext, zprev] + others
    for dev in partners:
        pl.semaphore_signal(bar, inc=1, device_id=dev, device_id_type=MESH)
    pl.semaphore_wait(bar, len(partners))

    def to_sib(p):
        return rc(panels[p].at[:, sib_cols], pan.at[p, own_at, :], sa_s.at[p], sa_r.at[p], sib)

    for p in range(3):
        to_sib(p).start()

    def region(p, zz, xx):
        return pan.at[p, pl.ds(pl.multiple_of((zz * 2 + xx) * blk, blk), blk), :]

    def psend(p, k, zz, xx, dev):
        ref = region(p, zz, xx)
        return rc(ref, ref, pan_s.at[p, k], pan_r.at[p, zz * 2 + xx], dev)

    def pwait(p, zz, xx):
        psend(p, 0, zz, xx, pair).wait_recv()

    def own_out(p):
        wlocal(p).wait()
        sib_at = pl.ds(pl.multiple_of((i + 1 - 2 * c) * own_rows, own_rows), own_rows)
        rc(panels[p].at[:, sib_cols], pan.at[p, sib_at, :], sa_s.at[p], sa_r.at[p], sib).wait_recv()
        psend(p, 0, z, x, pair).start()
        psend(p, 1, z, x, znext).start()
        psend(p, 2, z, x, zprev).start()

    def pair_on(p):
        pwait(p, z, ox)
        psend(p, 3, z, ox, znext).start()
        psend(p, 4, z, ox, zprev).start()

    def ring_on(p):
        pwait(p, zp, x)
        psend(p, 5, zp, x, znext).start()
        pwait(p, zn, ox)
        psend(p, 6, zn, ox, zprev).start()

    def panel_rest(p):
        pwait(p, zp, ox)
        pwait(p, zn, x)
        pwait(p, (z + 2) % RING, 0)
        pwait(p, (z + 2) % RING, 1)

    low, high = pl.ds(0, own_rows), pl.ds(own_rows, own_rows)

    def hsend(p, k, zz, n, dev):
        ref = region(p, zz, x).at[low if n == 0 else high, :]
        return rc(ref, ref, pan_s.at[p, k], half_r.at[n], dev)

    def first_ring(p):
        pwait(p, zp, x)
        hsend(p, 5, zp, 0, znext).start()
        psend(p, 3, zp, x, pair).start()
        pwait(p, zn, x)
        hsend(p, 6, zn, 1, zprev).start()
        psend(p, 4, zn, x, pair).start()

    def last_pair(p):
        z2 = (z + 2) % RING
        hsend(p, 5, z2, 0, znext).wait_recv()
        hsend(p, 6, z2, 1, zprev).wait_recv()
        psend(p, 7, z2, x, pair).start()

    def first_rest(p):
        for k in range(4):
            pwait(p, (z + k) % RING, ox)

    own_out(0)
    own_out(1)

    hit = asg[...] == 0
    routed = jnp.max(jnp.where(hit, 1.0, 0.0), axis=0, keepdims=True)
    weight = jnp.sum(jnp.where(hit, cmb[...], 0.0), axis=0, keepdims=True)
    before = lax.broadcasted_iota(jnp.int32, (toks, toks), 0)
    after = lax.broadcasted_iota(jnp.int32, (toks, toks), 1)
    upto = jnp.where(before <= after, 1.0, 0.0).astype(BF)
    place = nn(jnp.broadcast_to(routed, (8, toks)).astype(BF), upto)[0:1, :] - 1.0
    slot = lax.broadcasted_iota(jnp.int32, (rows, toks), 0).astype(F32)
    chosen = jnp.where(slot == place, routed, 0.0)
    rw = jnp.sum(chosen * weight, axis=1, keepdims=True)
    rwv[...] = jnp.broadcast_to(rw, rwv.shape)
    sel[...] = chosen.astype(BF)
    selt[...] = chosen.T.astype(BF)

    mine = pl.ds(pl.multiple_of(c * rows, rows), rows)
    theirs = pl.ds(pl.multiple_of(oc * rows, rows), rows)
    tiles = width // tile

    def rows_send(k, ref, at):
        return rc(ref.at[at, :], ref.at[at, :], row_s.at[k], row_r.at[k], sib)

    @pl.loop(0, tiles)
    def _(k):
        load(tok, k).wait()
        at = pl.ds(pl.multiple_of(k * tile, tile), tile)
        rin[mine, at] = nn(sel[...], tb[k % 2]).astype(BF)

        @pl.when(k + 2 < tiles)
        def _():
            load(tok, k + 2).start()

    rows_send(0, rin, mine).start()
    load(cot, 0).start()
    load(cot, 1).start()
    first_ring(0)
    pair_on(1)
    own_out(2)

    @pl.loop(0, tiles)
    def _(k):
        load(cot, k).wait()
        at = pl.ds(pl.multiple_of(k * tile, tile), tile)
        got = nn(sel[...], tb[k % 2])
        og[mine, at] = (rwv[:, 0:1] * got).astype(BF)

        @pl.when(k + 2 < tiles)
        def _():
            load(cot, k + 2).start()

    rows_send(1, og, mine).start()
    own_t = pl.ds(pl.multiple_of(t * cols, 128), cols)

    def load_cols():
        return pltpu.make_async_copy(cot.at[:, own_t], tb.at[0, :, pl.ds(0, cols)], ld_sem.at[0])

    load_cols().start()
    last_pair(0)
    ring_on(1)
    pair_on(2)

    third = 256
    steps = 2 * rows // third

    def rtile(k):
        return pl.ds(pl.multiple_of(k * third, third), third)

    rows_send(0, rin, theirs).wait_recv()
    first_rest(0)

    @pl.loop(0, steps)
    def _(k):
        gpre[rtile(k), :] = nn(rin[rtile(k), :], pan[0])

    ring_on(2)
    panel_rest(1)

    @pl.loop(0, steps)
    def _(k):
        u = nn(rin[rtile(k), :], pan[1])
        g = gpre[rtile(k), :]
        upre[rtile(k), :] = u
        hid[rtile(k), :] = (g * jax.nn.sigmoid(g) * u).astype(BF)

    rows_send(1, og, theirs).wait_recv()

    def chunk_at(j):
        return (z + 2 + 3 * j + 3 * (j // 2) + 2 * (j // 3)) % RING

    unit = half // 2

    def terms(p, left, right):
        tr[...] = left[...].T

        @pl.loop(0, RING)
        def _(j):
            q = chunk_at(j)
            at = pl.ds(pl.multiple_of(q * 2 * blk, 2 * blk), 2 * blk)
            got = nn(tr[...], right[:, at])
            for h in range(2):
                part = got[h * unit : (h + 1) * unit].astype(BF)
                grd[2 * p + h, q * 2] = part[:, :blk]
                grd[2 * p + h, q * 2 + 1] = part[:, blk:]

    def scatter(src, a1, a2, a3, ssem, rsem, q, pos, side, nxt, prv, mate, at):
        n1, p1, o2 = (pos + 1) % RING, (pos + 3) % RING, (pos + 2) % RING
        other = 1 - side

        def out(k, ref, dst, dev):
            return rc(ref, dst, ssem.at[q, k], rsem.at[q, k], dev)

        lanes = [
            out(0, src.at[q, at(o2, 0)], a1.at[q, 0], nxt),
            out(1, src.at[q, at(o2, 1)], a1.at[q, 1], prv),
            out(2, src.at[q, at(n1, 1)], a2.at[q, 0, 1], nxt),
            out(3, src.at[q, at(p1, 0)], a2.at[q, 1, 0], prv),
            out(4, src.at[q, at(n1, 0)], a2.at[q, 0, 0], nxt),
            out(5, src.at[q, at(p1, 1)], a2.at[q, 1, 1], prv),
            out(6, src.at[q, at(pos, other)], a3.at[q], mate),
        ]

        def got2(d, s):
            ref = a2.at[q, d, s]
            k = 2 + 2 * (1 - s) + d * (4 * s - 1)
            rc(ref, ref, ssem.at[q, 0], rsem.at[q, k], mate).wait_recv()
            return a2[q, d, s].astype(F32)

        def begin():
            for k in range(4):
                lanes[k].start()

        def middle():
            lanes[0].wait_recv()
            src[q, at(n1, 0)] = (src[q, at(n1, 0)].astype(F32) + a1[q, 0].astype(F32)).astype(BF)
            lanes[4].start()
            lanes[1].wait_recv()
            src[q, at(p1, 1)] = (src[q, at(p1, 1)].astype(F32) + a1[q, 1].astype(F32)).astype(BF)
            lanes[5].start()

        def over():
            total = src[q, at(pos, other)].astype(F32) + got2(0, other) + got2(1, other)
            src[q, at(pos, other)] = total.astype(BF)
            lanes[6].start()

        def finish():
            total = src[q, at(pos, side)].astype(F32) + got2(0, side) + got2(1, side)
            lanes[6].wait_recv()
            return total + a3[q].astype(F32)

        def drain():
            for copy in lanes:
                copy.wait_send()

        return begin, middle, over, finish, drain

    def scatter_pair(p, n):
        n1, p1, o2 = (z + 1) % RING, (z + 3) % RING, (z + 2) % RING
        chunks = (o2, n1, p1, z)
        cut = unit // 2
        top, bottom = slice(0, cut), slice(cut, 2 * cut)

        def out(k, ref, dst, dev):
            return rc(ref, dst, bs.at[n, k], br.at[n, k], dev)

        def own(q):
            return q * 2 + x

        lanes = [out(k, grd.at[p, q * 2 + ox], b1.at[n, k], pair) for k, q in enumerate(chunks)]
        lanes += [
            out(4, grd.at[p, own(o2), top, :], b2.at[n, 0], znext),
            out(5, grd.at[p, own(o2), bottom, :], b2.at[n, 1], zprev),
            out(6, grd.at[p, own(n1), bottom, :], b3.at[n, 0, bottom, :], znext),
            out(7, grd.at[p, own(p1), top, :], b3.at[n, 1, top, :], zprev),
            out(8, grd.at[p, own(n1), top, :], b3.at[n, 0, top, :], znext),
            out(9, grd.at[p, own(p1), bottom, :], b3.at[n, 1, bottom, :], zprev),
        ]

        def add(k, part, more):
            at = own(chunks[k])
            grd[p, at, part, :] = (grd[p, at, part, :].astype(F32) + more.astype(F32)).astype(BF)

        def begin():
            for k in range(4):
                lanes[k].start()

        def middle():
            lanes[0].wait_recv()
            add(0, slice(None), b1[n, 0])
            lanes[4].start()
            lanes[5].start()
            lanes[1].wait_recv()
            add(1, slice(None), b1[n, 1])
            lanes[6].start()
            lanes[2].wait_recv()
            add(2, slice(None), b1[n, 2])
            lanes[7].start()

        def over():
            lanes[4].wait_recv()
            add(1, top, b2[n, 0])
            lanes[8].start()
            lanes[5].wait_recv()
            add(2, bottom, b2[n, 1])
            lanes[9].start()

        def finish():
            lanes[3].wait_recv()
            total = grd[p, own(z)].astype(F32) + b1[n, 3].astype(F32)
            for k in (6, 8, 7, 9):
                lanes[k].wait_recv()
            return total + b3[n, 0].astype(F32) + b3[n, 1].astype(F32)

        def drain():
            for copy in lanes:
                copy.wait_send()

        return begin, middle, over, finish, drain

    def placed_at(a, b):
        return a * 2 + b

    def ring_grad(p, q):
        src = grd.at[p : p + 1]
        return scatter(
            src, r1.at[q : q + 1], r2.at[q : q + 1], r3.at[q : q + 1], gs.at[q : q + 1],
            gr.at[q : q + 1], 0, z, x, znext, zprev, pair, placed_at,
        )

    gate_a, gate_b, up_a, up_b, down_a, down_b = (
        ring_grad(0, 0), ring_grad(1, 1), scatter_pair(2, 0),
        ring_grad(3, 2), scatter_pair(4, 1), ring_grad(5, 3),
    )
    feats = [
        scatter(ub, u1, u2, u3, us, ur, q, y, xh, ynext, yprev, far, lambda a, b: b * RING + a)
        for q in range(2)
    ]

    terms(2, hid, og)
    down_a[0]()
    down_b[0]()

    def prow(p, j):
        return pan[p, pl.ds(pl.multiple_of(j * 2 * cols, 2 * cols), 2 * cols), :]

    def share(q, dst):
        return rc(dst, rx.at[q], xs.at[q], xr.at[q], sib)

    def down_chunk(q, first):
        at = pl.ds(pl.multiple_of(q * 2 * blk, 2 * blk), 2 * blk)

        @pl.loop(0, steps)
        def _(k):
            more = nn(og[rtile(k), at], pan[2, at, :])
            hgs[rtile(k), :] = more if first else hgs[rtile(k), :] + more

        got = nt(hid[theirs, :], prow(2, q))
        ub[1, 2 * q] = got[:, :cols].astype(BF)
        ub[1, 2 * q + 1] = got[:, cols:].astype(BF)

    down_chunk(z, True)
    pwait(2, zp, ox)
    down_chunk(zp, False)
    pwait(2, zn, x)
    down_chunk(zn, False)
    down_b[1]()
    pwait(2, (z + 2) % RING, 0)
    pwait(2, (z + 2) % RING, 1)
    down_chunk((z + 2) % RING, False)
    share(0, ub.at[1]).start()

    @pl.loop(0, steps)
    def _(k):
        hg = hgs[rtile(k), :]
        g = gpre[rtile(k), :]
        s = jax.nn.sigmoid(g)
        ggr[rtile(k), :] = (hg * upre[rtile(k), :] * s * (1.0 + g * (1.0 - s))).astype(BF)
        ugr[rtile(k), :] = (hg * g * s).astype(BF)

    terms(0, ggr, rin)
    gate_a[0]()
    share(0, ub.at[1]).wait_recv()

    @pl.loop(0, 4)
    def _(j):
        got = nt(hid[mine, :], prow(2, j))
        ub[0, 2 * j] = (got[:, :cols] + rx[0, 2 * j].astype(F32)).astype(BF)
        ub[0, 2 * j + 1] = (got[:, cols:] + rx[0, 2 * j + 1].astype(F32)).astype(BF)

    feats[0][0]()
    down_b[2]()
    gate_a[1]()
    gate_b[0]()
    down_a[1]()
    terms(1, ugr, rin)
    up_a[0]()
    up_b[0]()

    @pl.loop(0, 4)
    def _(j):
        got = nt(ggr[theirs, :], prow(0, j)) + nt(ugr[theirs, :], prow(1, j))
        rx[0, 2 * j] = got[:, :cols].astype(BF)
        rx[0, 2 * j + 1] = got[:, cols:].astype(BF)

    share(1, rx.at[0]).start()
    gate_a[2]()
    gate_b[1]()
    feats[0][1]()
    share(0, ub.at[1]).wait_send()
    share(1, rx.at[0]).wait_recv()

    @pl.loop(0, 4)
    def _(j):
        got = nt(ggr[mine, :], prow(0, j)) + nt(ugr[mine, :], prow(1, j))
        ub[1, 2 * j] = (got[:, :cols] + rx[1, 2 * j].astype(F32)).astype(BF)
        ub[1, 2 * j + 1] = (got[:, cols:] + rx[1, 2 * j + 1].astype(F32)).astype(BF)

    feats[1][0]()
    down_a[2]()
    gate_b[2]()
    up_b[1]()
    up_a[1]()
    for p in range(3):
        for k in range(5):
            psend(p, k, z, x, pair).wait_send()
    for k in range(5, 7):
        hsend(0, k, z, 0, znext).wait_send()
        psend(1, k, z, x, pair).wait_send()
        psend(2, k, z, x, pair).wait_send()
    psend(0, 7, z, x, pair).wait_send()

    own_part = pl.ds(pl.multiple_of(c * own_rows, own_rows), own_rows)
    sib_part = pl.ds(pl.multiple_of(oc * own_rows, own_rows), own_rows)

    def hand(p, at):
        return rc(pan.at[p, sib_part, :], fin.at[p, :, at], fs.at[p], fr.at[p], sib)

    def give(p, h, piece):
        pan[p, 0:blk, h * unit : (h + 1) * unit] = piece[3]().T.astype(BF)

    def hand_over(p):
        hand(p, own_cols).start()
        fin[p, :, own_cols] = pan[p, own_part, :]

    outs = (gg, gu, gd)

    def put(k, src, dst):
        return pltpu.make_async_copy(src, dst, o_sem.at[k])

    def put_mixed():
        return put(3, tb.at[1, :, pl.ds(0, cols)], mixed)

    def put_igrad():
        return put(4, tb.at[0, :, pl.ds(0, cols)], igrad)

    feats[0][2]()
    feats[1][1]()
    up_b[2]()
    up_a[2]()
    give(2, 0, down_a)
    give(2, 1, down_b)
    hand_over(2)

    e = feats[0][3]()
    mrow = (rwv[:, 0:1] * e).astype(BF)
    tb[1, :, 0:cols] = nn(selt[...], mrow).astype(BF)
    put_mixed().start()
    load_cols().wait()
    g = nn(sel[...], tb[0, :, 0:cols])
    w = jnp.sum(g * e, axis=1, keepdims=True)
    placed = jnp.sum(sel[...].astype(F32) * w, axis=0, keepdims=True)
    wx[t] = jnp.broadcast_to(placed, (8, toks))

    def tell(k, slot):
        return rc(wx.at[slot], wx.at[slot], ws.at[k], wr.at[slot], others[k - 1])

    for k in range(1, 8):
        tell(k, t).start()

    feats[1][2]()
    give(0, 0, gate_a)
    give(0, 1, gate_b)
    hand_over(0)
    give(1, 1, up_b)
    for k in range(1, 8):
        tell(k, (t + k) % 8).wait_recv()
    total = wx[0]
    for k in range(1, 8):
        total = total + wx[k]
    wgrad[...] = total
    give(1, 0, up_a)
    hand_over(1)
    irow = feats[1][3]().astype(BF)
    tb[0, :, 0:cols] = nn(selt[...], irow).astype(BF)
    put_igrad().start()
    for n, p in enumerate((2, 0, 1)):
        hand(p, sib_cols).wait_recv()
        put(n, fin.at[p], outs[p]).start()
    for p in range(3):
        to_sib(p).wait_send()
        hand(p, own_cols).wait_send()
    for piece in (gate_a, gate_b, up_a, up_b, down_a, down_b):
        piece[4]()
    for q in range(2):
        feats[q][4]()
    share(1, rx.at[0]).wait_send()
    rows_send(0, rin, mine).wait_send()
    rows_send(1, og, mine).wait_send()
    for k in range(1, 8):
        tell(k, t).wait_send()
    put_mixed().wait()
    put_igrad().wait()
    for n, p in enumerate((2, 0, 1)):
        put(n, fin.at[p], outs[p]).wait()


def hand_out(m, a, g, u, d, w, mo, ao, go, uo, do, wo, mb, ab, gb, ub, db, isem, osem):
    srcs, mids, dsts = (m, a, g, u, d), (mb, ab, gb, ub, db), (mo, ao, go, uo, do)
    into = [pltpu.make_async_copy(srcs[k], mids[k], isem.at[k]) for k in range(5)]
    back = [pltpu.make_async_copy(mids[k], dsts[k], osem.at[k]) for k in range(5)]
    for copy in into:
        copy.start()
    wo[...] = w[0, :]
    for k in range(5):
        into[k].wait()
        back[k].start()
    for copy in back:
        copy.wait()


def local(tokens, assign, combine, cotangent, w_gate, w_up, w_down_t):
    toks, width = tokens.shape
    rows = toks // 2
    own_rows, hidden = w_gate.shape
    half = hidden // 2
    blk = width // 8
    cols = width // 8
    dma = pltpu.SemaphoreType.DMA
    vm = pltpu.VMEM
    anyspace = pl.BlockSpec(memory_space=pl.ANY)
    inside = pl.BlockSpec(memory_space=pltpu.VMEM)
    results = pl.pallas_call(
        kernel,
        out_shape=(
            jax.ShapeDtypeStruct((toks, cols), BF),
            jax.ShapeDtypeStruct((toks, cols), BF),
            jax.ShapeDtypeStruct((8, toks), F32),
            jax.ShapeDtypeStruct((own_rows, hidden), BF),
            jax.ShapeDtypeStruct((own_rows, hidden), BF),
            jax.ShapeDtypeStruct((own_rows, hidden), BF),
        ),
        in_specs=[inside, inside] + [anyspace] * 5,
        out_specs=(anyspace, anyspace, inside, anyspace, anyspace, anyspace),
        scratch_shapes=[
            vm((rows, toks), BF),
            vm((toks, rows), BF),
            vm((rows, 128), F32),
            vm((2, toks, 512), BF),
            vm((2 * rows, width), BF),
            vm((2 * rows, width), BF),
            vm((3, width, half), BF),
            vm((2 * rows, half), F32),
            vm((2 * rows, half), F32),
            vm((2 * rows, half), BF),
            vm((2 * rows, half), BF),
            vm((2 * rows, half), BF),
            vm((half, 2 * rows), BF),
            vm((6, 8, half // 2, blk), BF),
            vm((4, 2, half // 2, blk), BF),
            vm((4, 2, 2, half // 2, blk), BF),
            vm((4, half // 2, blk), BF),
            vm((2, 4, half // 2, blk), BF),
            vm((2, 2, half // 4, blk), BF),
            vm((2, 2, half // 2, blk), BF),
            vm((3, own_rows, hidden), BF),
            vm((2, 8, rows, cols), BF),
            vm((2, 8, rows, cols), BF),
            vm((2, 2, rows, cols), BF),
            vm((2, 2, 2, rows, cols), BF),
            vm((2, rows, cols), BF),
            vm((8, 8, toks), F32),
            vm((2 * rows, half), F32),
            dma((2,)), dma((3,)), dma((5,)),
            dma((3,)), dma((3,)), dma((3, 8)), dma((3, 8)), dma((2,)), dma((2,)), dma((2,)),
            dma((4, 7)), dma((4, 7)), dma((2, 10)), dma((2, 10)), dma((2, 7)), dma((2, 7)),
            dma((3,)), dma((3,)), dma((2,)), dma((2,)), dma((8,)), dma((8,)),
        ],
        compiler_params=pltpu.CompilerParams(
            collective_id=0, has_side_effects=True, vmem_limit_bytes=62 * 1024 * 1024
        ),
    )(assign.T, combine.T, tokens, cotangent, w_gate, w_up, w_down_t)
    mixed, igrad, wgrad, gg, gu, gd = results
    kept = (mixed, igrad, gg, gu, gd)
    mixed, igrad, gg, gu, gd, wgrad = pl.pallas_call(
        hand_out,
        out_shape=tuple(jax.ShapeDtypeStruct(a.shape, a.dtype) for a in kept)
        + (jax.ShapeDtypeStruct((toks,), F32),),
        in_specs=[anyspace] * 5 + [inside],
        out_specs=(anyspace,) * 5 + (inside,),
        scratch_shapes=[vm(a.shape, a.dtype) for a in kept] + [dma((5,)), dma((5,))],
    )(*kept, wgrad)
    return mixed, igrad, wgrad, gg, gu, gd


def solution(mesh):
    return jax.shard_map(
        local,
        mesh=mesh,
        in_specs=(
            P("dp", None),
            P("dp", None),
            P("dp", None),
            P("dp", None),
            P("dp", "tensor"),
            P("dp", "tensor"),
            P("dp", "tensor"),
        ),
        out_specs=(
            P("dp", "tensor"),
            P("dp", "tensor"),
            P("dp"),
            P("dp", "tensor"),
            P("dp", "tensor"),
            P("dp", "tensor"),
        ),
        check_vma=False,
    )
```
